32 devices in a mesh: dom: 32 (over z, y, x, core).
Axes of the slice: x: 2, y: 2, z: 4, core: 2. Of those that a mesh axis runs over, the one named last changes fastest.
Arguments:
- start_state: float32 [504, 8192], P(None, 'dom'), may hold values from -6 to 6
- material: float32 [3, 8192], P(None, 'dom'), may hold values from 0.35 to 1.4
- geometry: float32 [3, 8192], P(None, 'dom'), may hold values from 0.6 to 1.6
- clusters: int32 [8192], P('dom'), may hold values from 0 to 1, as said below
- neighbours: int32 [4, 8192], P(None, 'dom'), may hold values from -1 to 8191, as said below
- orientation: int32 [4, 8192], P(None, 'dom'), may hold values from 0 to 11
- stiffness: float32 [3, 56, 56], replicated, may hold values from -0.75 to 0.75
- face_trace: float32 [4, 21, 56], replicated, may hold values from -0.75 to 0.75
- face_lift: float32 [4, 56, 21], replicated, may hold values from -1.25 to 1.25
- face_turns: float32 [3, 21, 21], replicated, may hold values from -1.25 to 1.25
- cotangent: float32 [504, 8192], P(None, 'dom'), may hold values from -0.27 to 0.27
Outputs:
- final_state: float32 [504, 8192], P(None, 'dom')
- material_grad: float32 [3, 8192], P(None, 'dom')
The draws below stay inside these ranges and needn't reach their ends.
Inputs may be any that keep to these rules, and one draw needn't show every extreme that they name: `clusters`: 1 marks a fine element; a device's block of 256 elements holds at most 128 fine ones, and some block holds exactly 128. `neighbours`: element n sits on device n // 256. A neighbour on another device is 1 to 4 devices away counted around the device cycle, or exactly half the cycle away. For every device and every such distance (up or down), at most 16 of the device's faces name elements there; on every device exactly 16 faces name elements half the cycle away.
All inputs are finite; a program needn't handle non-finite values.
Results may differ from the reference program's by a relative error of at most 0.0001.
Values sent between devices are 32-bit elements; how exact they have to be, the bound alone decides.
A program may use at most 192 MiB of HBM per device.

```python
import math
import jax
import jax.numpy as jnp
from jax import lax

VARS = 9
BASIS = 56
FACE_BASIS = 21
TERMS = 6
REACH = 4
E_DEV = 256
CAP = 16
FINE_DEV = 128
ELEMS = 8192


def block_ranks(key, blocks, length):
    keys = jax.random.split(key, blocks)
    order = jax.vmap(lambda subkey: jax.random.permutation(subkey, length))(keys)
    row_ids = jnp.arange(blocks)[:, None]
    return jnp.zeros((blocks, length), jnp.int32).at[row_ids, order].set(jnp.arange(length, dtype=jnp.int32)[None, :])


def draw_clusters(key, part):
    device_count = ELEMS // E_DEV
    key_start, key_order, key_pick = jax.random.split(jax.random.fold_in(key, 23), 3)
    band_start = jax.random.randint(key_start, (), 0, device_count)
    band_width = max(1, device_count // 8)
    in_band = (jnp.arange(device_count) - band_start) % device_count < band_width
    element_rank = block_ranks(key_order, device_count, E_DEV)
    sparse_pick = jax.random.randint(key_pick, (device_count, E_DEV), 0, 8) == 0
    fine_mask = (element_rank < FINE_DEV) & (in_band[:, None] | sparse_pick)
    return fine_mask.astype(jnp.int32).reshape(ELEMS)


def draw_neighbours(key, part):
    device_count = ELEMS // E_DEV
    face_count = 4 * E_DEV
    near_count = 2 * REACH
    lane_count = near_count + 1
    key_counts, key_full, key_order, key_far, key_edge = jax.random.split(jax.random.fold_in(key, 11), 5)
    counts = jax.random.randint(key_counts, (device_count, lane_count), CAP // 2, CAP + 1)
    full_lane = jax.random.randint(key_full, (device_count,), 0, near_count)
    lane_ids = jnp.arange(lane_count)[None, :]
    counts = jnp.where(lane_ids == full_lane[:, None], CAP, counts)
    counts = jnp.where(lane_ids == near_count, CAP, counts)
    face_rank = block_ranks(key_order, device_count, face_count)
    lane_pick = face_rank // CAP
    lane_slot = face_rank % CAP
    lane_clip = jnp.minimum(lane_pick, lane_count - 1)
    remote = (face_rank < lane_count * CAP) & (lane_slot < jnp.take_along_axis(counts, lane_clip, axis=1))
    offset = jnp.where(lane_clip < REACH, lane_clip + 1, jnp.where(lane_clip < near_count, -(lane_clip - REACH + 1), device_count // 2))
    device_ids = jnp.arange(device_count)[:, None]
    target = (device_ids + offset) % device_count
    far_pick = jax.random.randint(key_far, (device_count, face_count), 0, E_DEV)
    boundary = jax.random.randint(key_edge, (device_count, face_count), 0, 16) == 0
    remote_id = target * E_DEV + far_pick
    local_id = device_ids * E_DEV + far_pick
    neighbour_ids = jnp.where(remote, remote_id, jnp.where(boundary, -1, local_id))
    return neighbour_ids.reshape(device_count, 4, E_DEV).transpose(1, 0, 2).reshape(4, ELEMS).astype(jnp.int32)


def place_ends(values, own_key, smallest, high):
    longest = values.shape.index(max(values.shape))
    spots = []
    for shift in (0, 1):
        where = [jax.random.randint(jax.random.fold_in(own_key, axis), (), 0, length) for axis, length in enumerate(values.shape)]
        where[longest] = (where[longest] + shift) % values.shape[longest]
        spots.append(tuple(where))
    return values.at[spots[0]].set(smallest).at[spots[1]].set(high)


def levels(stream_key, dims, cuts, low, top_value):
    level = 1.0
    for position, shards_of in cuts:
        steps = jax.random.uniform(jax.random.fold_in(jax.random.fold_in(stream_key, 6), position), (shards_of,), jnp.float32, low / len(cuts), top_value / len(cuts))
        level = level * jnp.repeat(jnp.exp(steps), dims[position] // shards_of).reshape((-1,) + (1,) * (len(dims) - 1 - position))
    return level


def scatter_about(rng, shape, width, reach, cuts=(), kind=jnp.bfloat16):
    values = width * jax.random.normal(rng, shape, jnp.float32)
    if cuts:
        values = values * levels(rng, shape, cuts, -0.22, 0.18)
    return jnp.clip(values, -reach, reach).astype(kind)


def setup_inputs(seed: int = 0) -> dict:
    arg_keys = jax.random.split(jax.random.key(seed), 12)
    start_state = scatter_about(arg_keys[0], (VARS * BASIS, ELEMS), 1.0, 6.0, ((1, 32),), jnp.float32)
    material = jnp.clip(jnp.exp(math.log(1.4) - 1.3862944 * jax.random.uniform(arg_keys[1], (3, ELEMS), jnp.float32) ** levels(arg_keys[1], (3, ELEMS), ((1, 32),), -0.2, 0.2)), 0.35, 1.4)
    geometry = jnp.clip(jnp.exp(math.log(1.6) - 0.98082923 * jax.random.uniform(arg_keys[2], (3, ELEMS), jnp.float32) ** levels(arg_keys[2], (3, ELEMS), ((1, 32),), -0.2, 0.2)), 0.6, 1.6)
    clusters = draw_clusters(jax.random.fold_in(arg_keys[11], 71), 0)
    neighbours = draw_neighbours(jax.random.fold_in(arg_keys[11], 71), 0)
    orientation = place_ends(jax.random.randint(arg_keys[5], (4, ELEMS), 0, 12), jax.random.fold_in(arg_keys[5], 1), 0, 11).astype(jnp.int32)
    stiffness = scatter_about(arg_keys[6], (3, BASIS, BASIS), BASIS ** -0.5, 0.75, (), jnp.float32)
    face_trace = scatter_about(arg_keys[7], (4, FACE_BASIS, BASIS), BASIS ** -0.5, 0.75, (), jnp.float32)
    face_lift = scatter_about(arg_keys[8], (4, BASIS, FACE_BASIS), FACE_BASIS ** -0.5, 1.25, (), jnp.float32)
    face_turns = scatter_about(arg_keys[9], (3, FACE_BASIS, FACE_BASIS), FACE_BASIS ** -0.5, 1.25, (), jnp.float32)
    cotangent = scatter_about(arg_keys[10], (VARS * BASIS, ELEMS), 0.045, 0.27, ((1, 32),), jnp.float32)
    return {"start_state": start_state, "material": material, "geometry": geometry, "clusters": clusters, "neighbours": neighbours, "orientation": orientation, "stiffness": stiffness, "face_trace": face_trace, "face_lift": face_lift, "face_turns": face_turns, "cotangent": cotangent}


highest = lax.Precision.HIGHEST
dt_step = 0.5
root_third = 0.5773502691896258
face_normals = ((0.0, 0.0, -1.0), (0.0, -1.0, 0.0), (-1.0, 0.0, 0.0), (root_third, root_third, root_third))

def taylor_weights(start_time, length):
    weights = []
    factorial = 1.0
    for degree in range(TERMS):
        factorial = factorial * (degree + 1)
        weights.append(((start_time + length) ** (degree + 1) - start_time ** (degree + 1)) / factorial)
    return weights

def star_apply(along_x, along_y, along_z, lame_value, shear_value, inverse_density):
    longitudinal = lame_value + 2.0 * shear_value
    outputs = [-(longitudinal * along_x[6] + lame_value * along_y[7] + lame_value * along_z[8]), -(lame_value * along_x[6] + longitudinal * along_y[7] + lame_value * along_z[8]), -(lame_value * along_x[6] + lame_value * along_y[7] + longitudinal * along_z[8]), -shear_value * (along_x[7] + along_y[6]), -shear_value * (along_y[8] + along_z[7]), -shear_value * (along_x[8] + along_z[6]), -inverse_density * (along_x[0] + along_y[3] + along_z[5]), -inverse_density * (along_x[3] + along_y[1] + along_z[4]), -inverse_density * (along_x[5] + along_y[4] + along_z[2])]
    return jnp.stack(outputs)

def basis_apply(matrix, values):
    return jnp.einsum('bc,vce->vbe', matrix, values, precision=highest)

def basis_transposed(matrix, values):
    return jnp.einsum('cb,vce->vbe', matrix, values, precision=highest)

def time_derivative(values, mat_values, geometry, stiffness):
    pieces = [geometry[axis_no] * basis_apply(stiffness[axis_no], values) for axis_no in range(3)]
    return -star_apply(pieces[0], pieces[1], pieces[2], mat_values[0], mat_values[1], mat_values[2])

def predict(values, mat_values, geometry, stiffness, weight_sets):
    totals = [weights[0] * values for weights in weight_sets]
    current = values
    for degree in range(1, TERMS):
        current = time_derivative(current, mat_values, geometry, stiffness)
        totals = [partial_sum + weights[degree] * current for partial_sum, weights in zip(totals, weight_sets)]
    return totals

def face_traces(window, face_trace):
    traced = jnp.einsum('gjb,vbe->vjge', face_trace, window, precision=highest)
    return traced.reshape(traced.shape[0], traced.shape[1], -1)

def orient_apply(raw_faces, far_turns, face_turns):
    result = jnp.zeros_like(raw_faces)
    for turn_no in range(3):
        turned = jnp.einsum('ji,vie->vje', face_turns[turn_no], raw_faces, precision=highest)
        result = result + jnp.where(far_turns == turn_no, turned, 0.0)
    return result

def update(window, inner, outer, mat_values, geometry, stiffness, face_lift):
    elements = window.shape[2]
    pieces = [geometry[axis_no] * basis_transposed(stiffness[axis_no], window) for axis_no in range(3)]
    change = star_apply(pieces[0], pieces[1], pieces[2], mat_values[0], mat_values[1], mat_values[2])
    wave_speed = jnp.sqrt((mat_values[0] + 2.0 * mat_values[1]) * mat_values[2])
    for face_no in range(4):
        own_side = inner[:, :, face_no * elements:(face_no + 1) * elements]
        far_side = outer[:, :, face_no * elements:(face_no + 1) * elements]
        average = 0.5 * (own_side + far_side)
        normal = face_normals[face_no]
        face_flux = star_apply(normal[0] * geometry[0] * average, normal[1] * geometry[1] * average, normal[2] * geometry[2] * average, mat_values[0], mat_values[1], mat_values[2])
        face_flux = face_flux + 0.5 * wave_speed * (own_side - far_side)
        change = change - jnp.einsum('bj,vje->vbe', face_lift[face_no], face_flux, precision=highest)
    return change

def outer_traces(inner, neighbours, orientation, face_turns, elements):
    flat_neighbour = neighbours.reshape(-1)
    face_codes = orientation.reshape(-1)
    index = face_codes // 3 * elements + jnp.maximum(flat_neighbour, 0)
    raw_faces = jnp.take(inner, index, axis=2)
    raw_faces = jnp.where(flat_neighbour >= 0, raw_faces, 0.0)
    return orient_apply(raw_faces, face_codes % 3, face_turns)

def reference(start_state, material, geometry, clusters, neighbours, orientation, stiffness, face_trace, face_lift, face_turns, cotangent):
    elements = start_state.shape[1]
    values = start_state.reshape(VARS, BASIS, elements)
    fine_mask = clusters == 1
    weights_first = taylor_weights(0.0, 0.5 * dt_step)
    weights_later = taylor_weights(0.5 * dt_step, 0.5 * dt_step)

    def forward(mat_values):
        window_first, window_coarse = predict(values, mat_values, geometry, stiffness, [weights_first, weights_later])
        inner_first = face_traces(window_first, face_trace)
        outer_first = outer_traces(inner_first, neighbours, orientation, face_turns, elements)
        change_first = update(window_first, inner_first, outer_first, mat_values, geometry, stiffness, face_lift)
        middle = values + change_first
        window_fine = predict(middle, mat_values, geometry, stiffness, [weights_first])[0]
        window_second = jnp.where(fine_mask, window_fine, window_coarse)
        inner_second = face_traces(window_second, face_trace)
        outer_second = outer_traces(inner_second, neighbours, orientation, face_turns, elements)
        change_second = update(window_second, inner_second, outer_second, mat_values, geometry, stiffness, face_lift)
        return values + change_first + change_second
    final_values, pullback = jax.vjp(forward, material)
    material_grad = pullback(cotangent.reshape(VARS, BASIS, elements))[0]
    return (final_values.reshape(VARS * BASIS, elements), material_grad)
```

```python
import functools

import jax
import jax.numpy as jnp
from jax import lax
from jax.experimental import pallas as pl
from jax.experimental.pallas import tpu as pltpu
from jax.sharding import PartitionSpec as P

VARS = 9
TERMS = 6
REACH = 4
CAP = 16
LANES = 2 * REACH + 1
SLOTS = LANES * CAP
STEPS = TERMS - 1
f32, bf16 = jnp.float32, jnp.bfloat16

dt_step = 0.5
root_third = 0.5773502691896258
face_normals = (
    (0.0, 0.0, -1.0),
    (0.0, -1.0, 0.0),
    (-1.0, 0.0, 0.0),
    (root_third, root_third, root_third),
)


def taylor_weights(start_time, length):
    weights = []
    factorial = 1.0
    for degree in range(TERMS):
        factorial = factorial * (degree + 1)
        weights.append(
            ((start_time + length) ** (degree + 1) - start_time ** (degree + 1)) / factorial
        )
    return weights


A_W = taylor_weights(0.0, 0.5 * dt_step)
C_W = taylor_weights(0.5 * dt_step, 0.5 * dt_step)


def right3(x):
    high = x.astype(bf16).astype(f32)
    return jnp.concatenate([high, high, x - high], axis=0).astype(bf16)


def left3(ref):
    a = ref[...]
    k = a.shape[1] // 3
    high = a.astype(bf16).astype(f32)
    col = lax.broadcasted_iota(jnp.int32, a.shape, 1)
    return jnp.where((col >= k) & (col < 2 * k), a - high, high).astype(bf16)


def halves(x):
    high = x.astype(bf16)
    return high, (x - high.astype(f32)).astype(bf16)


def mm(a, b):
    return jnp.dot(a, b, preferred_element_type=f32)


def mm_t(a, b):
    return lax.dot_general(a, b, (((1,), (1,)), ((), ())), preferred_element_type=f32)


def add(*terms):
    total = None
    for t in terms:
        if t is not None:
            total = t if total is None else total + t
    return total


def times(a, b):
    return None if a is None or b is None else a * b


def star_q(a):
    return [
        a(0, 6),
        a(1, 7),
        a(2, 8),
        add(a(0, 7), a(1, 6)),
        add(a(1, 8), a(2, 7)),
        add(a(0, 8), a(2, 6)),
        add(a(0, 0), a(1, 3), a(2, 5)),
        add(a(0, 3), a(1, 1), a(2, 4)),
        add(a(0, 5), a(1, 4), a(2, 2)),
    ]


def star_rows(q, mat):
    lam, mu, rinv = mat
    spread = lam * add(q[0], q[1], q[2])
    rows = [add(spread, times(2.0 * mu, q[v])) for v in range(3)]
    rows += [times(mu, q[v]) for v in range(3, 6)]
    rows += [times(rinv, q[v]) for v in range(6, 9)]
    return rows


def star_back(z, mat):
    lam, mu, rinv = mat

    def normal(axis):
        own = z(axis, axis)
        if own is None:
            return None
        return lam * (z(axis, 0) + z(axis, 1) + z(axis, 2)) + 2.0 * mu * own

    return [
        times(rinv, z(0, 6)),
        times(rinv, z(1, 7)),
        times(rinv, z(2, 8)),
        times(rinv, add(z(0, 7), z(1, 6))),
        times(rinv, add(z(1, 8), z(2, 7))),
        times(rinv, add(z(0, 8), z(2, 6))),
        add(normal(0), times(mu, add(z(1, 3), z(2, 5)))),
        add(normal(1), times(mu, add(z(0, 3), z(2, 4)))),
        add(normal(2), times(mu, add(z(1, 4), z(0, 5)))),
    ]


def star_grads(r, q):
    g_lam = (r[0] + r[1] + r[2]) * add(q[0], q[1], q[2])
    g_mu = add(*[times(r[v], q[v]) for v in range(3)])
    g_mu = 2.0 * g_mu + 0.0
    g_mu = add(g_mu, *[times(r[v], q[v]) for v in range(3, 6)])
    g_r = add(*[times(r[v], q[v]) for v in range(6, 9)])
    return [jnp.sum(g, axis=0, keepdims=True) for g in (g_lam, g_mu, g_r)]


def rows_of(ref, count):
    return [ref[n : n + 1, :] for n in range(count)]


def blocks(ref, size, base=0):
    return [ref[base + v * size : base + (v + 1) * size, :] for v in range(VARS)]


def put(ref, values, base=0):
    size = values[0].shape[0]
    for v in range(VARS):
        ref[base + v * size : base + (v + 1) * size, :] = values[v]


def pieces(matrix, values, geo):
    size = values[0].shape[0]
    products = [mm(matrix, right3(x)) for x in values]
    return lambda axis, v: geo[axis] * products[v][axis * size : (axis + 1) * size]


def predict_steps(matrix, cur, mat, geo, q_ref, outs):
    size = cur.shape[0] // VARS
    for degree in range(1, TERMS):
        q = star_q(pieces(matrix, blocks(cur, size), geo))
        put(q_ref, q, (degree - 1) * VARS * size)
        new = star_rows(q, mat)
        put(cur, new)
        for ref, weights in outs:
            for v in range(VARS):
                rows = slice(v * size, (v + 1) * size)
                ref[rows, :] = ref[rows, :] + weights[degree] * new[v]


def predict_back(matrix_t, seed, cur, mat, geo, q_ref, grads, last):
    size = cur.shape[0] // VARS
    put(cur, [seed(STEPS, v) for v in range(VARS)])
    for degree in range(STEPS, 0, -1):
        r = blocks(cur, size)
        q = blocks(q_ref, size, (degree - 1) * VARS * size)
        grads = [a + b for a, b in zip(grads, star_grads(r, q))]
        if degree > last:
            back = star_back(pieces(matrix_t, r, geo), mat)
            put(cur, [back[v] + seed(degree - 1, v) for v in range(VARS)])
    return grads


def trace_faces(tr, window, own_ref, elems):
    size = window.shape[0] // VARS
    fb = tr.shape[0] // 4
    for v in range(VARS):
        t = mm(tr, right3(window[v * size : (v + 1) * size, :]))
        for g in range(4):
            own_ref[v * fb : (v + 1) * fb, g * elems : (g + 1) * elems] = t[g * fb : (g + 1) * fb]
    if own_ref.shape[0] > VARS * fb:
        own_ref[VARS * fb :, :] = jnp.zeros(
            (own_ref.shape[0] - VARS * fb, own_ref.shape[1]), f32
        )


def onehot(rows, row_index):
    at = lax.broadcasted_iota(jnp.int32, (rows, row_index.shape[1]), 0)
    return jnp.where(at == row_index, 1.0, 0.0).astype(bf16)


def serve_hot(arrived, g, elems):
    at = lax.broadcasted_iota(jnp.int32, (SLOTS, elems), 1) + (g * elems + 1)
    return jnp.where(at == arrived, 1.0, 0.0).astype(bf16)


def serve(own_ref, arr_ref, tx_ref, elems):
    arrived = arr_ref[:, 0:1]
    total = None
    for g in range(4):
        hot = serve_hot(arrived, g, elems)
        high, low = halves(own_ref[:, g * elems : (g + 1) * elems])
        part = mm_t(hot, high) + mm_t(hot, low)
        total = part if total is None else total + part
    tx_ref[...] = total


def padded_t(rx_ref):
    x = rx_ref[...]
    pad = -x.shape[0] % 128
    return jnp.concatenate([x, jnp.zeros((pad, x.shape[1]), f32)], axis=0).T


def masked3(x, turn_row):
    return right3(jnp.concatenate([jnp.where(turn_row == o, x, 0.0) for o in range(3)], axis=0))


def outer_faces(own_ref, rx_ref, idx_ref, slot_ref, turn_ref, tn, outer_ref, elems):
    fb = tn.shape[0]
    high, low = halves(own_ref[...])
    rx_high, rx_low = halves(padded_t(rx_ref))
    for f in range(4):
        hot = onehot(own_ref.shape[1], idx_ref[f : f + 1, :])
        hot_s = onehot(rx_high.shape[1], slot_ref[f : f + 1, :])
        raw = mm(high, hot) + mm(low, hot) + mm(rx_high, hot_s) + mm(rx_low, hot_s)
        turn = turn_ref[f : f + 1, :]
        for v in range(VARS):
            outer_ref[v * fb : (v + 1) * fb, f * elems : (f + 1) * elems] = mm(
                tn, masked3(raw[v * fb : (v + 1) * fb], turn)
            )


def face_block(ref, f, elems, fb):
    return [ref[v * fb : (v + 1) * fb, f * elems : (f + 1) * elems] for v in range(VARS)]


def face_q(f, own, far, geo):
    n = [s * g if s else None for s, g in zip(face_normals[f], geo)]
    mean = [0.5 * (a + b) for a, b in zip(own, far)]
    return n, star_q(lambda axis, v: times(n[axis], mean[v]))


def update(window, kt, lf, own_ref, outer_ref, mat, geo, q_ref, elems):
    size = window.shape[0] // VARS
    fb = lf.shape[1] // 12
    q = star_q(pieces(kt, blocks(window, size), geo))
    put(q_ref, q)
    change = [-x for x in star_rows(q, mat)]
    half_speed = 0.5 * jnp.sqrt((mat[0] + 2.0 * mat[1]) * mat[2])
    flux = [[] for _ in range(VARS)]
    for f in range(4):
        own, far = face_block(own_ref, f, elems, fb), face_block(outer_ref, f, elems, fb)
        rows = star_rows(face_q(f, own, far, geo)[1], mat)
        for v in range(VARS):
            jump = half_speed * (own[v] - far[v])
            flux[v].append(jump if rows[v] is None else jump - rows[v])
    return [c - mm(lf, right3(jnp.concatenate(x, axis=0))) for c, x in zip(change, flux)]


def update_back(
    seed, ks, lt, tnt, own_ref, outer_ref, q_ref, idx_ref, slot_ref, turn_ref,
    mat, geo, own_cot, tx_ref, elems,
):
    fb = lt.shape[0] // 4
    size = seed[0].shape[0]
    direct = [-x for x in star_back(pieces(ks, seed, geo), mat)]
    grads = [-g for g in star_grads(seed, blocks(q_ref, size))]
    lam, mu, rinv = mat
    speed = jnp.sqrt((lam + 2.0 * mu) * rinv)
    g_speed = jnp.zeros_like(lam)
    lifted = [-mm(lt, right3(s)) for s in seed]
    pad = own_cot.shape[0] - VARS * fb
    scattered, sent = None, None
    for f in range(4):
        own, far = face_block(own_ref, f, elems, fb), face_block(outer_ref, f, elems, fb)
        n, q = face_q(f, own, far, geo)
        r = [lifted[v][f * fb : (f + 1) * fb] for v in range(VARS)]
        grads = [a - b for a, b in zip(grads, star_grads(r, q))]
        jump = add(*[r[v] * (own[v] - far[v]) for v in range(VARS)])
        g_speed = g_speed + 0.5 * jnp.sum(jump, axis=0, keepdims=True)
        back = star_back(lambda axis, v: times(n[axis], r[v]), mat)
        turn = turn_ref[f : f + 1, :]
        raw = []
        for v in range(VARS):
            side = (0.5 * speed) * r[v]
            mean = jnp.zeros_like(side) if back[v] is None else -0.5 * back[v]
            own_cot[v * fb : (v + 1) * fb, f * elems : (f + 1) * elems] = mean + side
            raw.append(mm(tnt, masked3(mean - side, turn)))
        raw = jnp.concatenate(raw + [jnp.zeros((pad, elems), f32)], axis=0)
        high, low = halves(raw)
        hot = onehot(own_cot.shape[1], idx_ref[f : f + 1, :])
        hot_s = onehot(SLOTS, slot_ref[f : f + 1, :])
        part = mm_t(high, hot) + mm_t(low, hot)
        scattered = part if scattered is None else scattered + part
        part = mm_t(hot_s, high) + mm_t(hot_s, low)
        sent = part if sent is None else sent + part
    tx_ref[...] = sent
    own_cot[VARS * fb :, :] = jnp.zeros((pad, own_cot.shape[1]), f32)
    own_cot[...] = own_cot[...] + scattered
    grads = [
        grads[0] + g_speed * rinv / (2.0 * speed),
        grads[1] + g_speed * rinv / speed,
        grads[2] + g_speed * (lam + 2.0 * mu) / (2.0 * speed),
    ]
    return direct, grads


def faces_back(own_cot, rx_ref, arr_ref, trt, elems):
    fb = trt.shape[1] // 12
    arrived = arr_ref[:, 0:1]
    rx = padded_t(rx_ref)[:, :SLOTS]
    high, low = halves(rx)
    total = []
    for g in range(4):
        hot = serve_hot(arrived, g, elems)
        total.append(
            own_cot[:, g * elems : (g + 1) * elems] + mm(high, hot) + mm(low, hot)
        )
    return [
        mm(trt, right3(jnp.concatenate([t[v * fb : (v + 1) * fb] for t in total], axis=0)))
        for v in range(VARS)
    ]


def setup_kernel(lane_ref, want_ref, slot_ref, req_ref):
    elems = lane_ref.shape[1]
    at = lax.broadcasted_iota(jnp.int32, (16, elems), 0)
    col = lax.broadcasted_iota(jnp.int32, (16, elems), 1)
    carry = jnp.zeros((16, 1), jnp.int32)
    total = jnp.zeros((SLOTS, 1), jnp.int32)
    for f in range(4):
        lane = lane_ref[f : f + 1, :]
        hot = jnp.where(at == lane, 1, 0)
        run = hot
        shift = 1
        while shift < elems:
            run = run + jnp.where(col >= shift, pltpu.roll(run, shift, 1), 0)
            shift *= 2
        rank = jnp.sum((run + carry - 1) * hot, axis=0, keepdims=True)
        carry = carry + jnp.sum(hot, axis=1, keepdims=True)
        slot = jnp.where(lane < LANES, lane * CAP + rank, -1)
        slot_ref[f : f + 1, :] = slot
        rows = lax.broadcasted_iota(jnp.int32, (SLOTS, elems), 0)
        total = total + jnp.sum(
            jnp.where(rows == slot, want_ref[f : f + 1, :], 0), axis=1, keepdims=True
        )
    req_ref[...] = jnp.broadcast_to(total, req_ref.shape)


def first_kernel(state, mat_ref, geo_ref, ks_ref, tr_ref, arr, w1, wc, q1, own1, tx, cur):
    elems = state.shape[1]
    mat, geo = rows_of(mat_ref, 3), rows_of(geo_ref, 3)
    cur[...] = state[...]
    w1[...] = A_W[0] * state[...]
    wc[...] = C_W[0] * state[...]
    predict_steps(left3(ks_ref), cur, mat, geo, q1, [(w1, A_W), (wc, C_W)])
    trace_faces(left3(tr_ref), w1, own1, elems)
    serve(own1, arr, tx, elems)


def second_kernel(
    state, mat_ref, geo_ref, fine, ks_ref, kt_ref, tr_ref, lf_ref, tn_ref,
    w1, wc, own1, rx, arr, idx, slot, turn,
    middle, outer1, qu1, w2, q2, own2, tx, cur,
):
    elems = state.shape[1]
    mat, geo = rows_of(mat_ref, 3), rows_of(geo_ref, 3)
    outer_faces(own1, rx, idx, slot, turn, left3(tn_ref), outer1, elems)
    change = update(w1, left3(kt_ref), left3(lf_ref), own1, outer1, mat, geo, qu1, elems)
    size = state.shape[0] // VARS
    put(middle, [s + c for s, c in zip(blocks(state, size), change)])
    cur[...] = middle[...]
    w2[...] = A_W[0] * middle[...]
    predict_steps(left3(ks_ref), cur, mat, geo, q2, [(w2, A_W)])
    w2[...] = jnp.where(fine[...] > 0, w2[...], wc[...])
    trace_faces(left3(tr_ref), w2, own2, elems)
    serve(own2, arr, tx, elems)


def third_kernel(
    mat_ref, geo_ref, ks_ref, kt_ref, lf_ref, lt_ref, tn_ref, tnt_ref,
    middle, w2, own2, rx, idx, slot, turn, cot,
    final, direct, own_cot, tx, grad, outer2, qu2,
):
    elems = w2.shape[1]
    size = w2.shape[0] // VARS
    mat, geo = rows_of(mat_ref, 3), rows_of(geo_ref, 3)
    outer_faces(own2, rx, idx, slot, turn, left3(tn_ref), outer2, elems)
    change = update(w2, left3(kt_ref), left3(lf_ref), own2, outer2, mat, geo, qu2, elems)
    put(final, [s + c for s, c in zip(blocks(middle, size), change)])
    back, grads = update_back(
        blocks(cot, size), left3(ks_ref), left3(lt_ref), left3(tnt_ref), own2, outer2, qu2,
        idx, slot, turn, mat, geo, own_cot, tx, elems,
    )
    put(direct, back)
    grad[...] = jnp.concatenate(grads, axis=0)


def fourth_kernel(
    mat_ref, geo_ref, fine, ks_ref, kt_ref, lt_ref, tnt_ref, trt_ref,
    direct2, own_cot2, rx, arr, q2, cot, own1, outer1, qu1, idx, slot, turn, grad_in,
    direct1, coarse, own_cot1, tx, grad, cur, part,
):
    elems = cot.shape[1]
    size = cot.shape[0] // VARS
    mat, geo = rows_of(mat_ref, 3), rows_of(geo_ref, 3)
    is_fine = fine[...] > 0
    back = faces_back(own_cot2, rx, arr, left3(trt_ref), elems)
    for v, (b, d) in enumerate(zip(back, blocks(direct2, size))):
        rows = slice(v * size, (v + 1) * size)
        part[rows, :] = jnp.where(is_fine, b + d, 0.0)
        coarse[rows, :] = jnp.where(is_fine, 0.0, b + d)

    def seed(degree, v):
        return A_W[degree] * part[v * size : (v + 1) * size, :]

    grads = predict_back(
        left3(kt_ref), seed, cur, mat, geo, q2, rows_of(grad_in, 3), 0
    )
    seed1 = [a + b for a, b in zip(blocks(cot, size), blocks(cur, size))]
    back, more = update_back(
        seed1, left3(ks_ref), left3(lt_ref), left3(tnt_ref), own1, outer1, qu1,
        idx, slot, turn, mat, geo, own_cot1, tx, elems,
    )
    put(direct1, back)
    grad[...] = jnp.concatenate([a + b for a, b in zip(grads, more)], axis=0)


def fifth_kernel(
    mat_ref, geo_ref, kt_ref, trt_ref, direct1, coarse, own_cot1, rx, arr, q1, grad_in,
    grad, cur, part,
):
    elems = coarse.shape[1]
    size = coarse.shape[0] // VARS
    mat, geo = rows_of(mat_ref, 3), rows_of(geo_ref, 3)
    back = faces_back(own_cot1, rx, arr, left3(trt_ref), elems)
    put(part, [a + b for a, b in zip(back, blocks(direct1, size))])

    def seed(degree, v):
        rows = slice(v * size, (v + 1) * size)
        return A_W[degree] * part[rows, :] + C_W[degree] * coarse[rows, :]

    grads = predict_back(left3(kt_ref), seed, cur, mat, geo, q1, rows_of(grad_in, 3), 1)
    grad[...] = jnp.concatenate(grads, axis=0)


def exchange_kernel(devices, sign, src, dst, send_sems, recv_sems):
    me = lax.axis_index("dom")
    shifts = [n + 1 for n in range(REACH)] + [-(n + 1) for n in range(REACH)] + [devices // 2]
    barrier = pltpu.get_barrier_semaphore()
    peers = [lax.rem(me + sign * s + 2 * devices, devices) for s in shifts]
    for peer in peers:
        pl.semaphore_signal(
            barrier, inc=1, device_id=(peer,), device_id_type=pl.DeviceIdType.MESH
        )
    pl.semaphore_wait(barrier, LANES)
    copies = []
    for n in reversed(range(LANES)):
        rows = pl.ds(n * CAP, CAP)
        copy = pltpu.make_async_remote_copy(
            src_ref=src.at[rows],
            dst_ref=dst.at[rows],
            send_sem=send_sems.at[n],
            recv_sem=recv_sems.at[n],
            device_id=(peers[n],),
            device_id_type=pl.DeviceIdType.MESH,
        )
        copy.start()
        copies.append(copy)
    for copy in copies:
        copy.wait()


def exchange(x, devices, sign, number):
    return pl.pallas_call(
        functools.partial(exchange_kernel, devices, sign),
        out_shape=jax.ShapeDtypeStruct(x.shape, x.dtype),
        in_specs=[pl.BlockSpec(memory_space=pltpu.VMEM)],
        out_specs=pl.BlockSpec(memory_space=pltpu.VMEM),
        scratch_shapes=[
            pltpu.SemaphoreType.DMA((LANES,)),
            pltpu.SemaphoreType.DMA((LANES,)),
        ],
        compiler_params=pltpu.CompilerParams(collective_id=number, has_side_effects=True),
        name="exchange%d" % number,
    )(x)


def call(kernel, outs, scratch, *args):
    return pl.pallas_call(
        kernel,
        out_shape=[jax.ShapeDtypeStruct(s, d) for s, d in outs],
        in_specs=[pl.BlockSpec(memory_space=pltpu.VMEM)] * len(args),
        out_specs=[pl.BlockSpec(memory_space=pltpu.VMEM)] * len(outs),
        scratch_shapes=[pltpu.VMEM(s, f32) for s in scratch],
        compiler_params=pltpu.CompilerParams(vmem_limit_bytes=60000 * 1024),
        name=kernel.__name__,
    )(*args)


def triple(a):
    return jnp.concatenate([a, a, a], axis=1)


def body(
    start_state, material, geometry, clusters, neighbours, orientation,
    stiffness, face_trace, face_lift, face_turns, cotangent,
):
    rows, elems = start_state.shape
    basis = rows // VARS
    face_basis = face_trace.shape[1]
    devices = lax.axis_size("dom")
    me = lax.axis_index("dom")
    near = 2 * REACH
    fb = -(-face_basis // 8) * 8
    grow = fb - face_basis
    frows = -(-VARS * fb // 128) * 128

    present = neighbours >= 0
    owner = jnp.where(present, neighbours // elems, me)
    far_element = jnp.where(present, neighbours % elems, 0)
    source = orientation // 3 * elems + far_element
    remote = owner != me
    idx = jnp.where(present & ~remote, source, -1)
    distance = (owner - me) % devices
    lane = jnp.where(
        distance <= REACH,
        distance - 1,
        jnp.where(distance >= devices - REACH, REACH + devices - distance - 1, near),
    )
    lane = jnp.where(remote, lane, LANES)
    turn = orientation % 3
    want = source + 1
    fine = (clusters == 1).astype(jnp.int32).reshape(1, elems)

    ks = triple(stiffness.reshape(3 * basis, basis))
    kt = triple(stiffness.transpose(0, 2, 1).reshape(3 * basis, basis))
    trace = jnp.pad(face_trace, ((0, 0), (0, grow), (0, 0))).reshape(4 * fb, basis)
    lift = jnp.pad(face_lift, ((0, 0), (0, 0), (0, grow))).transpose(0, 2, 1)
    lift = lift.reshape(4 * fb, basis)
    turns = jnp.pad(face_turns, ((0, 0), (0, grow), (0, grow)))
    tr, trt = triple(trace), triple(trace.T)
    lt, lf = triple(lift), triple(lift.T)
    tn = triple(turns.transpose(1, 0, 2).reshape(fb, 3 * fb))
    tnt = triple(turns.transpose(2, 0, 1).reshape(fb, 3 * fb))

    full, faces, slots = (rows, elems), (frows, 4 * elems), (SLOTS, frows)
    hist, grads = (STEPS * rows, elems), (3, elems)
    F = lambda *shapes: [(s, f32) for s in shapes]

    slot, request = call(
        setup_kernel, [((4, elems), jnp.int32), ((SLOTS, 128), jnp.int32)], [], lane, want
    )
    arr = exchange(request, devices, 1, 0)
    w1, wc, q1, own1, tx = call(
        first_kernel, F(full, full, hist, faces, slots), [full],
        start_state, material, geometry, ks, tr, arr,
    )
    rx = exchange(tx, devices, -1, 1)
    middle, outer1, qu1, w2, q2, own2, tx = call(
        second_kernel, F(full, faces, full, full, hist, faces, slots), [full],
        start_state, material, geometry, fine, ks, kt, tr, lf, tn,
        w1, wc, own1, rx, arr, idx, slot, turn,
    )
    rx = exchange(tx, devices, -1, 2)
    final, direct2, own_cot2, tx, grad = call(
        third_kernel, F(full, full, faces, slots, grads), [faces, full],
        material, geometry, ks, kt, lf, lt, tn, tnt,
        middle, w2, own2, rx, idx, slot, turn, cotangent,
    )
    rx = exchange(tx, devices, 1, 3)
    direct1, coarse, own_cot1, tx, grad = call(
        fourth_kernel, F(full, full, faces, slots, grads), [full, full],
        material, geometry, fine, ks, kt, lt, tnt, trt,
        direct2, own_cot2, rx, arr, q2, cotangent, own1, outer1, qu1, idx, slot, turn, grad,
    )
    rx = exchange(tx, devices, 1, 4)
    (grad,) = call(
        fifth_kernel, F(grads), [full, full],
        material, geometry, kt, trt, direct1, coarse, own_cot1, rx, arr, q1, grad,
    )
    return (final, grad)


def solution(mesh):
    return jax.shard_map(
        body,
        mesh=mesh,
        in_specs=(
            P(None, "dom"),
            P(None, "dom"),
            P(None, "dom"),
            P("dom"),
            P(None, "dom"),
            P(None, "dom"),
            P(),
            P(),
            P(),
            P(),
            P(None, "dom"),
        ),
        out_specs=(P(None, "dom"), P(None, "dom")),
        check_vma=False,
    )
```

```python
import functools

import jax
import jax.numpy as jnp
from jax import lax
from jax.experimental import pallas as pl
from jax.experimental.pallas import tpu as pltpu
from jax.sharding import PartitionSpec as P

VARS = 9
TERMS = 6
REACH = 4
CAP = 16
LANES = 2 * REACH + 1
SLOTS = LANES * CAP
STEPS = TERMS - 1
f32, bf16 = jnp.float32, jnp.bfloat16

dt_step = 0.5
root_third = 0.5773502691896258
face_normals = (
    (0.0, 0.0, -1.0),
    (0.0, -1.0, 0.0),
    (-1.0, 0.0, 0.0),
    (root_third, root_third, root_third),
)


def taylor_weights(start_time, length):
    weights = []
    factorial = 1.0
    for degree in range(TERMS):
        factorial = factorial * (degree + 1)
        weights.append(
            ((start_time + length) ** (degree + 1) - start_time ** (degree + 1)) / factorial
        )
    return weights


A_W = taylor_weights(0.0, 0.5 * dt_step)
C_W = taylor_weights(0.5 * dt_step, 0.5 * dt_step)


def right3(x):
    high = x.astype(bf16).astype(f32)
    return jnp.concatenate([high, high, x - high], axis=0).astype(bf16)


def left3(ref):
    a = ref[...]
    k = a.shape[1] // 3
    high = a.astype(bf16).astype(f32)
    col = lax.broadcasted_iota(jnp.int32, a.shape, 1)
    return jnp.where((col >= k) & (col < 2 * k), a - high, high).astype(bf16)


def halves(x):
    high = x.astype(bf16)
    return high, (x - high.astype(f32)).astype(bf16)


def mm(a, b):
    return jnp.dot(a, b, preferred_element_type=f32)


def mm_t(a, b):
    return lax.dot_general(a, b, (((1,), (1,)), ((), ())), preferred_element_type=f32)


def add(*terms):
    total = None
    for t in terms:
        if t is not None:
            total = t if total is None else total + t
    return total


def times(a, b):
    return None if a is None or b is None else a * b


def star_q(a):
    return [
        a(0, 6),
        a(1, 7),
        a(2, 8),
        add(a(0, 7), a(1, 6)),
        add(a(1, 8), a(2, 7)),
        add(a(0, 8), a(2, 6)),
        add(a(0, 0), a(1, 3), a(2, 5)),
        add(a(0, 3), a(1, 1), a(2, 4)),
        add(a(0, 5), a(1, 4), a(2, 2)),
    ]


def star_rows(q, mat):
    lam, mu, rinv = mat
    spread = lam * add(q[0], q[1], q[2])
    rows = [add(spread, times(2.0 * mu, q[v])) for v in range(3)]
    rows += [times(mu, q[v]) for v in range(3, 6)]
    rows += [times(rinv, q[v]) for v in range(6, 9)]
    return rows


def star_back(z, mat):
    lam, mu, rinv = mat

    def normal(axis):
        own = z(axis, axis)
        if own is None:
            return None
        return lam * (z(axis, 0) + z(axis, 1) + z(axis, 2)) + 2.0 * mu * own

    return [
        times(rinv, z(0, 6)),
        times(rinv, z(1, 7)),
        times(rinv, z(2, 8)),
        times(rinv, add(z(0, 7), z(1, 6))),
        times(rinv, add(z(1, 8), z(2, 7))),
        times(rinv, add(z(0, 8), z(2, 6))),
        add(normal(0), times(mu, add(z(1, 3), z(2, 5)))),
        add(normal(1), times(mu, add(z(0, 3), z(2, 4)))),
        add(normal(2), times(mu, add(z(1, 4), z(0, 5)))),
    ]


def star_grads(r, q):
    g_lam = (r[0] + r[1] + r[2]) * add(q[0], q[1], q[2])
    g_mu = add(*[times(r[v], q[v]) for v in range(3)])
    g_mu = 2.0 * g_mu + 0.0
    g_mu = add(g_mu, *[times(r[v], q[v]) for v in range(3, 6)])
    g_r = add(*[times(r[v], q[v]) for v in range(6, 9)])
    return [jnp.sum(g, axis=0, keepdims=True) for g in (g_lam, g_mu, g_r)]


def rows_of(ref, count):
    return [ref[n : n + 1, :] for n in range(count)]


def blocks(ref, size, base=0):
    return [ref[base + v * size : base + (v + 1) * size, :] for v in range(VARS)]


def put(ref, values, base=0):
    size = values[0].shape[0]
    for v in range(VARS):
        ref[base + v * size : base + (v + 1) * size, :] = values[v]


def pieces(matrix, values, geo):
    size = values[0].shape[0]
    products = [mm(matrix, right3(x)) for x in values]
    return lambda axis, v: geo[axis] * products[v][axis * size : (axis + 1) * size]


def predict_steps(matrix, cur, mat, geo, q_ref, outs):
    size = cur.shape[0] // VARS
    for degree in range(1, TERMS):
        q = star_q(pieces(matrix, blocks(cur, size), geo))
        put(q_ref, q, (degree - 1) * VARS * size)
        new = star_rows(q, mat)
        put(cur, new)
        for ref, weights in outs:
            for v in range(VARS):
                rows = slice(v * size, (v + 1) * size)
                ref[rows, :] = ref[rows, :] + weights[degree] * new[v]


def back_step(matrix_t, r, mat, geo):
    return star_back(pieces(matrix_t, r, geo), mat)


def chain_grads(hist_ref, q_ref, size, grads):
    for degree in range(STEPS):
        base = degree * VARS * size
        more = star_grads(blocks(hist_ref, size, base), blocks(q_ref, size, base))
        grads = [a + b for a, b in zip(grads, more)]
    return grads


def trace_faces(tr, window, own_ref, elems):
    size = window.shape[0] // VARS
    fb = tr.shape[0] // 4
    for v in range(VARS):
        t = mm(tr, right3(window[v * size : (v + 1) * size, :]))
        for g in range(4):
            own_ref[v * fb : (v + 1) * fb, g * elems : (g + 1) * elems] = t[g * fb : (g + 1) * fb]
    if own_ref.shape[0] > VARS * fb:
        own_ref[VARS * fb :, :] = jnp.zeros(
            (own_ref.shape[0] - VARS * fb, own_ref.shape[1]), f32
        )


def onehot(rows, row_index):
    at = lax.broadcasted_iota(jnp.int32, (rows, row_index.shape[1]), 0)
    return jnp.where(at == row_index, 1.0, 0.0).astype(bf16)


def serve_hot(arrived, g, elems):
    at = lax.broadcasted_iota(jnp.int32, (SLOTS, elems), 1) + (g * elems + 1)
    return jnp.where(at == arrived, 1.0, 0.0).astype(bf16)


def serve(own_ref, arr_ref, tx_ref, elems):
    arrived = arr_ref[:, arr_ref.shape[1] - 1 :].astype(jnp.int32)
    total = None
    for g in range(4):
        hot = serve_hot(arrived, g, elems)
        high, low = halves(own_ref[:, g * elems : (g + 1) * elems])
        part = mm_t(hot, high) + mm_t(hot, low)
        total = part if total is None else total + part
    tx_ref[...] = total


def padded_t(rx_ref):
    x = rx_ref[...]
    pad = -x.shape[0] % 128
    return jnp.concatenate([x, jnp.zeros((pad, x.shape[1]), f32)], axis=0).T


def masked3(x, turn_row):
    return right3(jnp.concatenate([jnp.where(turn_row == o, x, 0.0) for o in range(3)], axis=0))


def local_faces(own_ref, idx_ref, raw_ref, elems):
    high, low = halves(own_ref[...])
    for f in range(4):
        hot = onehot(own_ref.shape[1], idx_ref[f : f + 1, :])
        raw_ref[:, f * elems : (f + 1) * elems] = mm(high, hot) + mm(low, hot)


def outer_faces(raw_ref, rx_ref, slot_ref, turn_ref, tn, outer_ref, elems):
    fb = tn.shape[0]
    rx_high, rx_low = halves(padded_t(rx_ref))
    for f in range(4):
        cols = slice(f * elems, (f + 1) * elems)
        hot_s = onehot(rx_high.shape[1], slot_ref[f : f + 1, :])
        raw = raw_ref[:, cols] + mm(rx_high, hot_s) + mm(rx_low, hot_s)
        turn = turn_ref[f : f + 1, :]
        for v in range(VARS):
            outer_ref[v * fb : (v + 1) * fb, cols] = mm(
                tn, masked3(raw[v * fb : (v + 1) * fb], turn)
            )


def face_block(ref, f, elems, fb):
    return [ref[v * fb : (v + 1) * fb, f * elems : (f + 1) * elems] for v in range(VARS)]


def face_q(f, own, far, geo):
    n = [s * g if s else None for s, g in zip(face_normals[f], geo)]
    mean = [0.5 * (a + b) for a, b in zip(own, far)]
    return n, star_q(lambda axis, v: times(n[axis], mean[v]))


def volume(window, kt, mat, geo, q_ref, change_ref):
    size = window.shape[0] // VARS
    q = star_q(pieces(kt, blocks(window, size), geo))
    put(q_ref, q)
    put(change_ref, [-x for x in star_rows(q, mat)])


def surface(lf, own_ref, outer_ref, mat, geo, elems):
    fb = lf.shape[1] // 12
    half_speed = 0.5 * jnp.sqrt((mat[0] + 2.0 * mat[1]) * mat[2])
    flux = [[] for _ in range(VARS)]
    for f in range(4):
        own, far = face_block(own_ref, f, elems, fb), face_block(outer_ref, f, elems, fb)
        rows = star_rows(face_q(f, own, far, geo)[1], mat)
        for v in range(VARS):
            jump = half_speed * (own[v] - far[v])
            flux[v].append(jump if rows[v] is None else jump - rows[v])
    return [-mm(lf, right3(jnp.concatenate(x, axis=0))) for x in flux]


def update_back(
    seed, ks, lt, tnt, idx_ref, slot_ref, turn_ref, mat, geo, own_cot, tx_ref, elems
):
    fb = lt.shape[0] // 4
    direct = [-x for x in star_back(pieces(ks, seed, geo), mat)]
    lam, mu, rinv = mat
    half_speed = 0.5 * jnp.sqrt((lam + 2.0 * mu) * rinv)
    lifted = [-mm(lt, right3(s)) for s in seed]
    pad = own_cot.shape[0] - VARS * fb
    scattered, sent = None, None
    for f in range(4):
        n = [s * g if s else None for s, g in zip(face_normals[f], geo)]
        r = [lifted[v][f * fb : (f + 1) * fb] for v in range(VARS)]
        back = star_back(lambda axis, v: times(n[axis], r[v]), mat)
        turn = turn_ref[f : f + 1, :]
        raw = []
        for v in range(VARS):
            side = half_speed * r[v]
            mean = jnp.zeros_like(side) if back[v] is None else -0.5 * back[v]
            own_cot[v * fb : (v + 1) * fb, f * elems : (f + 1) * elems] = mean + side
            raw.append(mm(tnt, masked3(mean - side, turn)))
        raw = jnp.concatenate(raw + [jnp.zeros((pad, elems), f32)], axis=0)
        high, low = halves(raw)
        hot = onehot(own_cot.shape[1], idx_ref[f : f + 1, :])
        hot_s = onehot(SLOTS, slot_ref[f : f + 1, :])
        part = mm_t(high, hot) + mm_t(low, hot)
        scattered = part if scattered is None else scattered + part
        part = mm_t(hot_s, high) + mm_t(hot_s, low)
        sent = part if sent is None else sent + part
    tx_ref[...] = sent
    own_cot[VARS * fb :, :] = jnp.zeros((pad, own_cot.shape[1]), f32)
    own_cot[...] = own_cot[...] + scattered
    return direct


def update_grads(seed, lt, own_ref, outer_ref, q_ref, mat, geo, elems):
    fb = lt.shape[0] // 4
    grads = [-g for g in star_grads(seed, blocks(q_ref, seed[0].shape[0]))]
    lam, mu, rinv = mat
    speed = jnp.sqrt((lam + 2.0 * mu) * rinv)
    g_speed = jnp.zeros_like(lam)
    lifted = [-mm(lt, right3(s)) for s in seed]
    for f in range(4):
        own, far = face_block(own_ref, f, elems, fb), face_block(outer_ref, f, elems, fb)
        q = face_q(f, own, far, geo)[1]
        r = [lifted[v][f * fb : (f + 1) * fb] for v in range(VARS)]
        grads = [a - b for a, b in zip(grads, star_grads(r, q))]
        jump = add(*[r[v] * (own[v] - far[v]) for v in range(VARS)])
        g_speed = g_speed + 0.5 * jnp.sum(jump, axis=0, keepdims=True)
    return [
        grads[0] + g_speed * rinv / (2.0 * speed),
        grads[1] + g_speed * rinv / speed,
        grads[2] + g_speed * (lam + 2.0 * mu) / (2.0 * speed),
    ]


def faces_back(own_cot, rx_ref, arr_ref, trt, elems):
    fb = trt.shape[1] // 12
    arrived = arr_ref[:, arr_ref.shape[1] - 1 :].astype(jnp.int32)
    rx = padded_t(rx_ref)[:, :SLOTS]
    high, low = halves(rx)
    total = []
    for g in range(4):
        hot = serve_hot(arrived, g, elems)
        total.append(
            own_cot[:, g * elems : (g + 1) * elems] + mm(high, hot) + mm(low, hot)
        )
    return [
        mm(trt, right3(jnp.concatenate([t[v * fb : (v + 1) * fb] for t in total], axis=0)))
        for v in range(VARS)
    ]


def peers_of(devices):
    me = lax.axis_index("dom")
    shifts = [n + 1 for n in range(REACH)] + [-(n + 1) for n in range(REACH)] + [devices // 2]
    return [
        [lax.rem(me + sign * s + 2 * devices, devices) for s in shifts] for sign in (1, -1)
    ]


def greet(peers):
    barrier = pltpu.get_barrier_semaphore()
    for peer in peers:
        pl.semaphore_signal(
            barrier, inc=1, device_id=(peer,), device_id_type=pl.DeviceIdType.MESH
        )
    pl.semaphore_wait(barrier, LANES)


def send_all(peers, src, dst, send_sems, recv_sems, base=0):
    copies = []
    for n in reversed(range(LANES)):
        rows = pl.ds(n * CAP, CAP)
        copy = pltpu.make_async_remote_copy(
            src_ref=src.at[rows],
            dst_ref=dst.at[rows],
            send_sem=send_sems.at[base + n],
            recv_sem=recv_sems.at[base + n],
            device_id=(peers[n],),
            device_id_type=pl.DeviceIdType.MESH,
        )
        copy.start()
        copies.append(copy)
    return copies


def start_kernel(
    lane_ref, want_ref, idx, turn, mat_ref, geo_ref, ks_ref, lt_ref, tnt_ref, cot,
    slot_ref, direct, own_cot, tx,
):
    elems = lane_ref.shape[1]
    at = lax.broadcasted_iota(jnp.int32, (16, elems), 0)
    col = lax.broadcasted_iota(jnp.int32, (16, elems), 1)
    carry = jnp.zeros((16, 1), jnp.int32)
    total = jnp.zeros((SLOTS, 1), jnp.int32)
    for f in range(4):
        lane = lane_ref[f : f + 1, :]
        hot = jnp.where(at == lane, 1, 0)
        run = hot
        shift = 1
        while shift < elems:
            run = run + jnp.where(col >= shift, pltpu.roll(run, shift, 1), 0)
            shift *= 2
        rank = jnp.sum((run + carry - 1) * hot, axis=0, keepdims=True)
        carry = carry + jnp.sum(hot, axis=1, keepdims=True)
        slot = jnp.where(lane < LANES, lane * CAP + rank, -1)
        slot_ref[f : f + 1, :] = slot
        rows = lax.broadcasted_iota(jnp.int32, (SLOTS, elems), 0)
        total = total + jnp.sum(
            jnp.where(rows == slot, want_ref[f : f + 1, :], 0), axis=1, keepdims=True
        )
    mat, geo = rows_of(mat_ref, 3), rows_of(geo_ref, 3)
    size = cot.shape[0] // VARS
    put(direct, update_back(
        blocks(cot, size), left3(ks_ref), left3(lt_ref), left3(tnt_ref), idx, slot_ref, turn,
        mat, geo, own_cot, tx, elems,
    ))
    last = lax.broadcasted_iota(jnp.int32, tx.shape, 1) == tx.shape[1] - 1
    tx[...] = jnp.where(last, total.astype(f32), tx[...])


def first_kernel(
    devices, src, state, mat_ref, geo_ref, ks_ref, tr_ref,
    rx, w1, wc, q1, own1, tx, cur, send_sems, recv_sems,
):
    up, down = peers_of(devices)
    greet(up)
    copies = send_all(up, src, rx, send_sems, recv_sems)
    elems = state.shape[1]
    mat, geo = rows_of(mat_ref, 3), rows_of(geo_ref, 3)
    cur[...] = state[...]
    w1[...] = A_W[0] * state[...]
    wc[...] = C_W[0] * state[...]
    predict_steps(left3(ks_ref), cur, mat, geo, q1, [(w1, A_W), (wc, C_W)])
    trace_faces(left3(tr_ref), w1, own1, elems)
    for copy in copies:
        copy.wait()
    serve(own1, rx, tx, elems)


def second_kernel(
    devices, src, state, cot, mat_ref, geo_ref, fine,
    ks_ref, kt_ref, tr_ref, trt_ref, lf_ref, lt_ref, tn_ref, tnt_ref,
    direct2, own_cot2, rx0, w1, wc, own1, idx, slot, turn,
    middle, outer1, qu1, w2, q2, own2, tx, hist, seed1, coarse, direct1, own_cot1, tx_cot,
    cur, part, raw, rx, send_sems, recv_sems,
):
    up, down = peers_of(devices)
    greet(down)
    copies = send_all(down, src, rx, send_sems, recv_sems)
    elems = state.shape[1]
    size = state.shape[0] // VARS
    mat, geo = rows_of(mat_ref, 3), rows_of(geo_ref, 3)
    ks, kt = left3(ks_ref), left3(kt_ref)
    is_fine = fine[...] > 0
    back = faces_back(own_cot2, rx0, rx0, left3(trt_ref), elems)
    for v, (b, d) in enumerate(zip(back, blocks(direct2, size))):
        rows = slice(v * size, (v + 1) * size)
        part[rows, :] = jnp.where(is_fine, b + d, 0.0)
        coarse[rows, :] = jnp.where(is_fine, 0.0, b + d)
    put(hist, [A_W[STEPS] * x for x in blocks(part, size)], (STEPS - 1) * VARS * size)
    for degree in range(STEPS, 0, -1):
        r = back_step(kt, blocks(hist, size, (degree - 1) * VARS * size), mat, geo)
        r = [a + A_W[degree - 1] * b for a, b in zip(r, blocks(part, size))]
        if degree > 1:
            put(hist, r, (degree - 2) * VARS * size)
        else:
            put(seed1, [a + b for a, b in zip(r, blocks(cot, size))])
    put(direct1, update_back(
        blocks(seed1, size), ks, left3(lt_ref), left3(tnt_ref), idx, slot, turn,
        mat, geo, own_cot1, tx_cot, elems,
    ))
    local_faces(own1, idx, raw, elems)
    volume(w1, kt, mat, geo, qu1, middle)
    for copy in copies:
        copy.wait()
    outer_faces(raw, rx, slot, turn, left3(tn_ref), outer1, elems)
    change = surface(left3(lf_ref), own1, outer1, mat, geo, elems)
    put(middle, [
        s + m + c for s, m, c in zip(blocks(state, size), blocks(middle, size), change)
    ])
    cur[...] = middle[...]
    w2[...] = A_W[0] * middle[...]
    predict_steps(ks, cur, mat, geo, q2, [(w2, A_W)])
    w2[...] = jnp.where(is_fine, w2[...], wc[...])
    trace_faces(left3(tr_ref), w2, own2, elems)
    serve(own2, rx0, tx, elems)


def third_kernel(
    devices, src, src_cot, cot, mat_ref, geo_ref, kt_ref, trt_ref, lf_ref, lt_ref, tn_ref,
    middle, w2, own2, q2, hist, own1, outer1, qu1, q1, seed1, coarse, direct1, own_cot1,
    rx0, idx, slot, turn,
    final, grad, outer2, qu2, raw, cur, part, rx, rx_cot, send_sems, recv_sems,
):
    up, down = peers_of(devices)
    greet(up)
    copies = send_all(up, src_cot, rx_cot, send_sems, recv_sems)
    copies += send_all(down, src, rx, send_sems, recv_sems, LANES)
    elems = w2.shape[1]
    size = w2.shape[0] // VARS
    mat, geo = rows_of(mat_ref, 3), rows_of(geo_ref, 3)
    kt, lt = left3(kt_ref), left3(lt_ref)
    local_faces(own2, idx, raw, elems)
    volume(w2, kt, mat, geo, qu2, final)
    grads = update_grads(blocks(seed1, size), lt, own1, outer1, qu1, mat, geo, elems)
    grads = chain_grads(hist, q2, size, grads)
    for copy in copies:
        copy.wait()
    outer_faces(raw, rx, slot, turn, left3(tn_ref), outer2, elems)
    change = surface(left3(lf_ref), own2, outer2, mat, geo, elems)
    put(final, [
        s + m + c for s, m, c in zip(blocks(middle, size), blocks(final, size), change)
    ])
    more = update_grads(blocks(cot, size), lt, own2, outer2, qu2, mat, geo, elems)
    grads = [a + b for a, b in zip(grads, more)]
    back = faces_back(own_cot1, rx_cot, rx0, left3(trt_ref), elems)
    put(part, [a + b for a, b in zip(back, blocks(direct1, size))])
    for degree in range(STEPS, 0, -1):
        own_part = [
            A_W[degree] * a + C_W[degree] * b
            for a, b in zip(blocks(part, size), blocks(coarse, size))
        ]
        if degree < STEPS:
            r = back_step(kt, blocks(cur, size), mat, geo)
            own_part = [a + b for a, b in zip(r, own_part)]
        put(cur, own_part)
        q = blocks(q1, size, (degree - 1) * VARS * size)
        grads = [a + b for a, b in zip(grads, star_grads(blocks(cur, size), q))]
    grad[...] = jnp.concatenate(grads, axis=0)


def call(kernel, outs, scratch, *args, number=None, copies=0, devices=None):
    extra, name = {}, kernel.__name__
    sems = []
    if number is not None:
        extra = dict(collective_id=number, has_side_effects=True)
        sems = [pltpu.SemaphoreType.DMA((copies,))] * 2
        kernel = functools.partial(kernel, devices)
    return pl.pallas_call(
        kernel,
        out_shape=[jax.ShapeDtypeStruct(s, d) for s, d in outs],
        in_specs=[pl.BlockSpec(memory_space=pltpu.VMEM)] * len(args),
        out_specs=[pl.BlockSpec(memory_space=pltpu.VMEM)] * len(outs),
        scratch_shapes=[pltpu.VMEM(s, f32) for s in scratch] + sems,
        compiler_params=pltpu.CompilerParams(vmem_limit_bytes=60000 * 1024, **extra),
        name=name,
    )(*args)


def triple(a):
    return jnp.concatenate([a, a, a], axis=1)


def body(
    start_state, material, geometry, clusters, neighbours, orientation,
    stiffness, face_trace, face_lift, face_turns, cotangent,
):
    rows, elems = start_state.shape
    basis = rows // VARS
    face_basis = face_trace.shape[1]
    devices = lax.axis_size("dom")
    me = lax.axis_index("dom")
    near = 2 * REACH
    fb = -(-face_basis // 8) * 8
    grow = fb - face_basis
    frows = -(-VARS * fb // 128) * 128

    present = neighbours >= 0
    owner = jnp.where(present, neighbours // elems, me)
    far_element = jnp.where(present, neighbours % elems, 0)
    source = orientation // 3 * elems + far_element
    remote = owner != me
    idx = jnp.where(present & ~remote, source, -1)
    distance = (owner - me) % devices
    lane = jnp.where(
        distance <= REACH,
        distance - 1,
        jnp.where(distance >= devices - REACH, REACH + devices - distance - 1, near),
    )
    lane = jnp.where(remote, lane, LANES)
    turn = orientation % 3
    want = source + 1
    fine = (clusters == 1).astype(jnp.int32).reshape(1, elems)

    ks = triple(stiffness.reshape(3 * basis, basis))
    kt = triple(stiffness.transpose(0, 2, 1).reshape(3 * basis, basis))
    trace = jnp.pad(face_trace, ((0, 0), (0, grow), (0, 0))).reshape(4 * fb, basis)
    lift = jnp.pad(face_lift, ((0, 0), (0, 0), (0, grow))).transpose(0, 2, 1)
    lift = lift.reshape(4 * fb, basis)
    turns = jnp.pad(face_turns, ((0, 0), (0, grow), (0, grow)))
    tr, trt = triple(trace), triple(trace.T)
    lt, lf = triple(lift), triple(lift.T)
    tn = triple(turns.transpose(1, 0, 2).reshape(fb, 3 * fb))
    tnt = triple(turns.transpose(2, 0, 1).reshape(fb, 3 * fb))

    full, faces, slots = (rows, elems), (frows, 4 * elems), (SLOTS, frows)
    hist, grads = (STEPS * rows, elems), (3, elems)
    F = lambda *shapes: [(s, f32) for s in shapes]

    slot, direct2, own_cot2, tx = call(
        start_kernel, [((4, elems), jnp.int32)] + F(full, faces, slots), [],
        lane, want, idx, turn, material, geometry, ks, lt, tnt, cotangent,
    )
    rx0, w1, wc, q1, own1, tx = call(
        first_kernel, F(slots, full, full, hist, faces, slots), [full],
        tx, start_state, material, geometry, ks, tr,
        number=0, copies=LANES, devices=devices,
    )
    (
        middle, outer1, qu1, w2, q2, own2, tx, back, seed1, coarse, direct1, own_cot1, tx_cot
    ) = call(
        second_kernel,
        F(full, faces, full, full, hist, faces, slots, hist, full, full, full, faces, slots),
        [full, full, faces, slots],
        tx, start_state, cotangent, material, geometry, fine,
        ks, kt, tr, trt, lf, lt, tn, tnt,
        direct2, own_cot2, rx0, w1, wc, own1, idx, slot, turn,
        number=1, copies=LANES, devices=devices,
    )
    final, grad = call(
        third_kernel, F(full, grads), [faces, full, faces, full, full, slots, slots],
        tx, tx_cot, cotangent, material, geometry, kt, trt, lf, lt, tn,
        middle, w2, own2, q2, back, own1, outer1, qu1, q1, seed1, coarse, direct1, own_cot1,
        rx0, idx, slot, turn,
        number=2, copies=2 * LANES, devices=devices,
    )
    return (final, grad)


def solution(mesh):
    return jax.shard_map(
        body,
        mesh=mesh,
        in_specs=(
            P(None, "dom"),
            P(None, "dom"),
            P(None, "dom"),
            P("dom"),
            P(None, "dom"),
            P(None, "dom"),
            P(),
            P(),
            P(),
            P(),
            P(None, "dom"),
        ),
        out_specs=(P(None, "dom"), P(None, "dom")),
        check_vma=False,
    )
```

```python
import functools

import jax
import jax.numpy as jnp
from jax import lax
from jax.experimental import pallas as pl
from jax.experimental.pallas import tpu as pltpu
from jax.sharding import PartitionSpec as P

VARS = 9
TERMS = 6
REACH = 4
CAP = 16
LANES = 2 * REACH + 1
SLOTS = LANES * CAP
STEPS = TERMS - 1
f32, bf16 = jnp.float32, jnp.bfloat16

dt_step = 0.5
root_third = 0.5773502691896258
face_normals = (
    (0.0, 0.0, -1.0),
    (0.0, -1.0, 0.0),
    (-1.0, 0.0, 0.0),
    (root_third, root_third, root_third),
)


def taylor_weights(start_time, length):
    weights = []
    factorial = 1.0
    for degree in range(TERMS):
        factorial = factorial * (degree + 1)
        weights.append(
            ((start_time + length) ** (degree + 1) - start_time ** (degree + 1)) / factorial
        )
    return weights


A_W = taylor_weights(0.0, 0.5 * dt_step)
C_W = taylor_weights(0.5 * dt_step, 0.5 * dt_step)


def right3(x):
    high = x.astype(bf16).astype(f32)
    return jnp.concatenate([high, high, x - high], axis=0).astype(bf16)


def left3(a):
    high = a.astype(bf16).astype(f32)
    return jnp.concatenate([high, a - high, high], axis=1).astype(bf16)


def halves(x):
    high = x.astype(bf16)
    return high, (x - high.astype(f32)).astype(bf16)


def mm(a, b):
    return jnp.dot(a, b, preferred_element_type=f32)


def mm_t(a, b):
    return lax.dot_general(a, b, (((1,), (1,)), ((), ())), preferred_element_type=f32)


def add(*terms):
    total = None
    for t in terms:
        if t is not None:
            total = t if total is None else total + t
    return total


def times(a, b):
    return None if a is None or b is None else a * b


def star_q(a):
    return [
        a(0, 6),
        a(1, 7),
        a(2, 8),
        add(a(0, 7), a(1, 6)),
        add(a(1, 8), a(2, 7)),
        add(a(0, 8), a(2, 6)),
        add(a(0, 0), a(1, 3), a(2, 5)),
        add(a(0, 3), a(1, 1), a(2, 4)),
        add(a(0, 5), a(1, 4), a(2, 2)),
    ]


def star_rows(q, mat):
    lam, mu, rinv = mat
    spread = lam * add(q[0], q[1], q[2])
    rows = [add(spread, times(2.0 * mu, q[v])) for v in range(3)]
    rows += [times(mu, q[v]) for v in range(3, 6)]
    rows += [times(rinv, q[v]) for v in range(6, 9)]
    return rows


def star_back(z, mat):
    lam, mu, rinv = mat

    def normal(axis):
        own = z(axis, axis)
        if own is None:
            return None
        return lam * (z(axis, 0) + z(axis, 1) + z(axis, 2)) + 2.0 * mu * own

    return [
        times(rinv, z(0, 6)),
        times(rinv, z(1, 7)),
        times(rinv, z(2, 8)),
        times(rinv, add(z(0, 7), z(1, 6))),
        times(rinv, add(z(1, 8), z(2, 7))),
        times(rinv, add(z(0, 8), z(2, 6))),
        add(normal(0), times(mu, add(z(1, 3), z(2, 5)))),
        add(normal(1), times(mu, add(z(0, 3), z(2, 4)))),
        add(normal(2), times(mu, add(z(1, 4), z(0, 5)))),
    ]


def star_grads(r, q):
    g_lam = (r[0] + r[1] + r[2]) * add(q[0], q[1], q[2])
    g_mu = add(*[times(r[v], q[v]) for v in range(3)])
    g_mu = 2.0 * g_mu + 0.0
    g_mu = add(g_mu, *[times(r[v], q[v]) for v in range(3, 6)])
    g_r = add(*[times(r[v], q[v]) for v in range(6, 9)])
    return [jnp.sum(g, axis=0, keepdims=True) for g in (g_lam, g_mu, g_r)]


def rows_of(ref, count):
    return [ref[n : n + 1, :] for n in range(count)]


def blocks(ref, size, base=0):
    return [ref[base + v * size : base + (v + 1) * size, :] for v in range(VARS)]


def put(ref, values, base=0):
    size = values[0].shape[0]
    for v in range(VARS):
        ref[base + v * size : base + (v + 1) * size, :] = values[v]


def pieces(matrix, values, geo):
    size = values[0].shape[0]
    products = [mm(matrix, right3(x)) for x in values]
    return lambda axis, v: geo[axis] * products[v][axis * size : (axis + 1) * size]


def predict_steps(matrix, cur, mat, geo, q_ref, outs):
    size = cur.shape[0] // VARS
    for degree in range(1, TERMS):
        q = star_q(pieces(matrix, blocks(cur, size), geo))
        put(q_ref, q, (degree - 1) * VARS * size)
        new = star_rows(q, mat)
        put(cur, new)
        for ref, weights in outs:
            for v in range(VARS):
                rows = slice(v * size, (v + 1) * size)
                ref[rows, :] = ref[rows, :] + weights[degree] * new[v]


def back_step(matrix_t, r, mat, geo):
    return star_back(pieces(matrix_t, r, geo), mat)


def chain_grads(hist_ref, q_ref, size, grads):
    for degree in range(STEPS):
        base = degree * VARS * size
        more = star_grads(blocks(hist_ref, size, base), blocks(q_ref, size, base))
        grads = [a + b for a, b in zip(grads, more)]
    return grads


def trace_faces(tr, window, own_ref, elems):
    size = window.shape[0] // VARS
    fb = tr.shape[0] // 4
    for v in range(VARS):
        t = mm(tr, right3(window[v * size : (v + 1) * size, :]))
        for g in range(4):
            own_ref[v * fb : (v + 1) * fb, g * elems : (g + 1) * elems] = t[g * fb : (g + 1) * fb]
    if own_ref.shape[0] > VARS * fb:
        own_ref[VARS * fb :, :] = jnp.zeros(
            (own_ref.shape[0] - VARS * fb, own_ref.shape[1]), f32
        )


def onehot(rows, row_index):
    at = lax.broadcasted_iota(jnp.int32, (rows, row_index.shape[1]), 0)
    return jnp.where(at == row_index, 1.0, 0.0).astype(bf16)


def serve_hot(arrived, g, elems):
    at = lax.broadcasted_iota(jnp.int32, (SLOTS, elems), 1) + (g * elems + 1)
    return jnp.where(at == arrived, 1.0, 0.0).astype(bf16)


def serve(own_ref, arr_ref, tx_ref, elems):
    arrived = arr_ref[:, arr_ref.shape[1] - 1 :].astype(jnp.int32)
    total = None
    for g in range(4):
        hot = serve_hot(arrived, g, elems)
        high, low = halves(own_ref[:, g * elems : (g + 1) * elems])
        part = mm_t(hot, high) + mm_t(hot, low)
        total = part if total is None else total + part
    tx_ref[...] = total


def padded_t(rx_ref):
    x = rx_ref[...]
    pad = -x.shape[0] % 128
    return jnp.concatenate([x, jnp.zeros((pad, x.shape[1]), f32)], axis=0).T


def masked3(x, turn_row):
    return right3(jnp.concatenate([jnp.where(turn_row == o, x, 0.0) for o in range(3)], axis=0))


def local_faces(own_ref, idx_ref, raw_ref, elems):
    high, low = halves(own_ref[...])
    for f in range(4):
        hot = onehot(own_ref.shape[1], idx_ref[f : f + 1, :])
        raw_ref[:, f * elems : (f + 1) * elems] = mm(high, hot) + mm(low, hot)


def outer_faces(raw_ref, rx_ref, slot_ref, turn_ref, tn, outer_ref, elems):
    fb = tn.shape[0]
    rx_high, rx_low = halves(padded_t(rx_ref))
    for f in range(4):
        cols = slice(f * elems, (f + 1) * elems)
        hot_s = onehot(rx_high.shape[1], slot_ref[f : f + 1, :])
        raw = raw_ref[:, cols] + mm(rx_high, hot_s) + mm(rx_low, hot_s)
        turn = turn_ref[f : f + 1, :]
        for v in range(VARS):
            outer_ref[v * fb : (v + 1) * fb, cols] = mm(
                tn, masked3(raw[v * fb : (v + 1) * fb], turn)
            )


def face_block(ref, f, elems, fb):
    return [ref[v * fb : (v + 1) * fb, f * elems : (f + 1) * elems] for v in range(VARS)]


def face_q(f, own, far, geo):
    n = [s * g if s else None for s, g in zip(face_normals[f], geo)]
    mean = [0.5 * (a + b) for a, b in zip(own, far)]
    return n, star_q(lambda axis, v: times(n[axis], mean[v]))


def volume(window, kt, mat, geo, q_ref, change_ref):
    size = window.shape[0] // VARS
    q = star_q(pieces(kt, blocks(window, size), geo))
    put(q_ref, q)
    put(change_ref, [-x for x in star_rows(q, mat)])


def surface(lf, own_ref, outer_ref, mat, geo, elems):
    fb = lf.shape[1] // 12
    half_speed = 0.5 * jnp.sqrt((mat[0] + 2.0 * mat[1]) * mat[2])
    flux = [[] for _ in range(VARS)]
    for f in range(4):
        own, far = face_block(own_ref, f, elems, fb), face_block(outer_ref, f, elems, fb)
        rows = star_rows(face_q(f, own, far, geo)[1], mat)
        for v in range(VARS):
            jump = half_speed * (own[v] - far[v])
            flux[v].append(jump if rows[v] is None else jump - rows[v])
    return [-mm(lf, right3(jnp.concatenate(x, axis=0))) for x in flux]


def volume_back(seed, ks, mat, geo):
    return [-x for x in star_back(pieces(ks, seed, geo), mat)]


def faces_cot(seed, lt, tnt, idx_ref, slot_ref, turn_ref, mat, geo, own_cot, tx_ref, elems):
    fb = lt.shape[0] // 4
    lam, mu, rinv = mat
    half_speed = 0.5 * jnp.sqrt((lam + 2.0 * mu) * rinv)
    lifted = [-mm(lt, right3(s)) for s in seed]
    pad = own_cot.shape[0] - VARS * fb
    scattered, sent = None, None
    for f in range(4):
        n = [s * g if s else None for s, g in zip(face_normals[f], geo)]
        r = [lifted[v][f * fb : (f + 1) * fb] for v in range(VARS)]
        back = star_back(lambda axis, v: times(n[axis], r[v]), mat)
        turn = turn_ref[f : f + 1, :]
        raw = []
        for v in range(VARS):
            side = half_speed * r[v]
            mean = jnp.zeros_like(side) if back[v] is None else -0.5 * back[v]
            own_cot[v * fb : (v + 1) * fb, f * elems : (f + 1) * elems] = mean + side
            raw.append(mm(tnt, masked3(mean - side, turn)))
        raw = jnp.concatenate(raw + [jnp.zeros((pad, elems), f32)], axis=0)
        high, low = halves(raw)
        hot = onehot(own_cot.shape[1], idx_ref[f : f + 1, :])
        hot_s = onehot(SLOTS, slot_ref[f : f + 1, :])
        part = mm_t(high, hot) + mm_t(low, hot)
        scattered = part if scattered is None else scattered + part
        part = mm_t(hot_s, high) + mm_t(hot_s, low)
        sent = part if sent is None else sent + part
    tx_ref[...] = sent
    own_cot[VARS * fb :, :] = jnp.zeros((pad, own_cot.shape[1]), f32)
    own_cot[...] = own_cot[...] + scattered


def update_grads(seed, lt, own_ref, outer_ref, q_ref, mat, geo, elems):
    fb = lt.shape[0] // 4
    grads = [-g for g in star_grads(seed, blocks(q_ref, seed[0].shape[0]))]
    lam, mu, rinv = mat
    speed = jnp.sqrt((lam + 2.0 * mu) * rinv)
    g_speed = jnp.zeros_like(lam)
    lifted = [-mm(lt, right3(s)) for s in seed]
    for f in range(4):
        own, far = face_block(own_ref, f, elems, fb), face_block(outer_ref, f, elems, fb)
        q = face_q(f, own, far, geo)[1]
        r = [lifted[v][f * fb : (f + 1) * fb] for v in range(VARS)]
        grads = [a - b for a, b in zip(grads, star_grads(r, q))]
        jump = add(*[r[v] * (own[v] - far[v]) for v in range(VARS)])
        g_speed = g_speed + 0.5 * jnp.sum(jump, axis=0, keepdims=True)
    return [
        grads[0] + g_speed * rinv / (2.0 * speed),
        grads[1] + g_speed * rinv / speed,
        grads[2] + g_speed * (lam + 2.0 * mu) / (2.0 * speed),
    ]


def faces_back(own_cot, rx_ref, arr_ref, trt, elems):
    fb = trt.shape[1] // 12
    arrived = arr_ref[:, arr_ref.shape[1] - 1 :].astype(jnp.int32)
    rx = padded_t(rx_ref)[:, :SLOTS]
    high, low = halves(rx)
    total = []
    for g in range(4):
        hot = serve_hot(arrived, g, elems)
        total.append(
            own_cot[:, g * elems : (g + 1) * elems] + mm(high, hot) + mm(low, hot)
        )
    return [
        mm(trt, right3(jnp.concatenate([t[v * fb : (v + 1) * fb] for t in total], axis=0)))
        for v in range(VARS)
    ]


def peers_of(devices):
    me = lax.axis_index("dom")
    shifts = [n + 1 for n in range(REACH)] + [-(n + 1) for n in range(REACH)] + [devices // 2]
    return [
        [lax.rem(me + sign * s + 2 * devices, devices) for s in shifts] for sign in (1, -1)
    ]


def send_all(peers, src, dst, send_sems, recv_sems, base=0):
    copies = []
    for n in reversed(range(LANES)):
        rows = pl.ds(n * CAP, CAP)
        copy = pltpu.make_async_remote_copy(
            src_ref=src.at[rows],
            dst_ref=dst.at[rows],
            send_sem=send_sems.at[base + n],
            recv_sem=recv_sems.at[base + n],
            device_id=(peers[n],),
            device_id_type=pl.DeviceIdType.MESH,
        )
        copy.start()
        copies.append(copy)
    return copies


def face_places(neighbours, orientation, devices, idx_ref, slot_ref, turn_ref):
    elems = neighbours.shape[1]
    me = lax.axis_index("dom")
    at = lax.broadcasted_iota(jnp.int32, (16, elems), 0)
    col = lax.broadcasted_iota(jnp.int32, (16, elems), 1)
    rows = lax.broadcasted_iota(jnp.int32, (SLOTS, elems), 0)
    carry = jnp.zeros((16, 1), jnp.int32)
    total = jnp.zeros((SLOTS, 1), jnp.int32)
    for f in range(4):
        name, code = neighbours[f : f + 1, :], orientation[f : f + 1, :]
        far_face = sum(jnp.where(code >= 3 * g, 1, 0) for g in (1, 2, 3))
        turn_ref[f : f + 1, :] = code - 3 * far_face
        present = name >= 0
        safe = jnp.maximum(name, 0)
        owner = jnp.floor((safe.astype(f32) + 0.5) * (1.0 / elems)).astype(jnp.int32)
        source = far_face * elems + safe - owner * elems
        away = owner - me
        away = jnp.where(away < 0, away + devices, away)
        idx_ref[f : f + 1, :] = jnp.where(present & (away == 0), source, -1)
        lane = jnp.where(
            away <= REACH,
            away - 1,
            jnp.where(away >= devices - REACH, REACH + devices - away - 1, 2 * REACH),
        )
        lane = jnp.where(present & (away != 0), lane, LANES)
        hot = jnp.where(at == lane, 1, 0)
        run = hot
        shift = 1
        while shift < elems:
            run = run + jnp.where(col >= shift, pltpu.roll(run, shift, 1), 0)
            shift *= 2
        rank = jnp.sum((run + carry - 1) * hot, axis=0, keepdims=True)
        carry = carry + jnp.sum(hot, axis=1, keepdims=True)
        slot = jnp.where(lane < LANES, lane * CAP + rank, -1)
        slot_ref[f : f + 1, :] = slot
        total = total + jnp.sum(jnp.where(rows == slot, source + 1, 0), axis=1, keepdims=True)
    return total


def stacked(blocks_in, scratch):
    scratch[...] = jnp.zeros(scratch.shape, f32)
    for n, x in enumerate(blocks_in):
        scratch[n, : x.shape[0], : x.shape[1]] = x
    return jnp.concatenate([scratch[n] for n in range(scratch.shape[0])], axis=0)


def step_kernel(
    devices,
    state, cot, mat_ref, geo_ref, fine, neighbours, orientation, stiffness, face_trace,
    face_lift, face_turns,
    final, grad,
    w1, wc, w2, cur, part, middle, coarse, seed1, direct1, direct2, qu1, qu2,
    q1, q2, hist, own1, own2, own_cot1, own_cot2, raw, outer1, outer2,
    tx0, tx1, tx2, tx3, rx0, rx1, rx2, rx3, trace_pad, lift_pad, turn_pad, turn_pad_t,
    idx, slot, turn, send_sems, recv_sems,
):
    up, down = peers_of(devices)
    barrier = pltpu.get_barrier_semaphore()
    for peer in up:
        pl.semaphore_signal(
            barrier, inc=1, device_id=(peer,), device_id_type=pl.DeviceIdType.MESH
        )
    elems = state.shape[1]
    size = state.shape[0] // VARS
    mat, geo = rows_of(mat_ref, 3), rows_of(geo_ref, 3)
    total = face_places(neighbours, orientation, devices, idx, slot, turn)

    stiff = [stiffness[d] for d in range(3)]
    ks = left3(jnp.concatenate(stiff, axis=0))
    kt = left3(jnp.concatenate([x.T for x in stiff], axis=0))
    trace = stacked([face_trace[g] for g in range(4)], trace_pad)
    lift = stacked([face_lift[f].T for f in range(4)], lift_pad)
    tr, trt, lt, lf = left3(trace), left3(trace.T), left3(lift), left3(lift.T)
    tnt = left3(stacked([face_turns[o] for o in range(3)], turn_pad).T)
    tn = left3(stacked([face_turns[o].T for o in range(3)], turn_pad_t).T)

    seed2 = blocks(cot, size)
    faces_cot(seed2, lt, tnt, idx, slot, turn, mat, geo, own_cot2, tx0, elems)
    last = lax.broadcasted_iota(jnp.int32, tx0.shape, 1) == tx0.shape[1] - 1
    tx0[...] = jnp.where(last, total.astype(f32), tx0[...])
    cur[...] = state[...]
    w1[...] = A_W[0] * state[...]
    wc[...] = C_W[0] * state[...]
    pl.semaphore_wait(barrier, LANES)
    sent0 = send_all(up, tx0, rx0, send_sems, recv_sems, 0)

    predict_steps(ks, cur, mat, geo, q1, [(w1, A_W), (wc, C_W)])
    trace_faces(tr, w1, own1, elems)
    local_faces(own1, idx, raw, elems)
    volume(w1, kt, mat, geo, qu1, middle)
    put(direct2, volume_back(seed2, ks, mat, geo))
    for copy in sent0:
        copy.wait()

    serve(own1, rx0, tx1, elems)
    back = faces_back(own_cot2, rx0, rx0, trt, elems)
    is_fine = fine[...] == 1
    for v, (b, d) in enumerate(zip(back, blocks(direct2, size))):
        rows = slice(v * size, (v + 1) * size)
        part[rows, :] = jnp.where(is_fine, b + d, 0.0)
        coarse[rows, :] = jnp.where(is_fine, 0.0, b + d)
    sent1 = send_all(down, tx1, rx1, send_sems, recv_sems, LANES)

    put(hist, [A_W[STEPS] * x for x in blocks(part, size)], (STEPS - 1) * VARS * size)
    for degree in range(STEPS, 0, -1):
        r = back_step(kt, blocks(hist, size, (degree - 1) * VARS * size), mat, geo)
        r = [a + A_W[degree - 1] * b for a, b in zip(r, blocks(part, size))]
        if degree > 1:
            put(hist, r, (degree - 2) * VARS * size)
        else:
            put(seed1, [a + b for a, b in zip(r, blocks(cot, size))])
    faces_cot(
        blocks(seed1, size), lt, tnt, idx, slot, turn, mat, geo, own_cot1, tx3, elems
    )
    put(direct1, volume_back(blocks(seed1, size), ks, mat, geo))
    sent3 = send_all(up, tx3, rx3, send_sems, recv_sems, 2 * LANES)
    for copy in sent1:
        copy.wait()

    outer_faces(raw, rx1, slot, turn, tn, outer1, elems)
    change = surface(lf, own1, outer1, mat, geo, elems)
    put(middle, [
        s + m + c for s, m, c in zip(blocks(state, size), blocks(middle, size), change)
    ])
    cur[...] = middle[...]
    w2[...] = A_W[0] * middle[...]
    predict_steps(ks, cur, mat, geo, q2, [(w2, A_W)])
    w2[...] = jnp.where(is_fine, w2[...], wc[...])
    trace_faces(tr, w2, own2, elems)
    serve(own2, rx0, tx2, elems)
    local_faces(own2, idx, raw, elems)
    sent2 = send_all(down, tx2, rx2, send_sems, recv_sems, 3 * LANES)

    volume(w2, kt, mat, geo, qu2, final)
    grads = update_grads(blocks(seed1, size), lt, own1, outer1, qu1, mat, geo, elems)
    grads = chain_grads(hist, q2, size, grads)
    for copy in sent3:
        copy.wait()
    back = faces_back(own_cot1, rx3, rx0, trt, elems)
    put(part, [a + b for a, b in zip(back, blocks(direct1, size))])
    for degree in range(STEPS, 0, -1):
        r = [
            A_W[degree] * a + C_W[degree] * b
            for a, b in zip(blocks(part, size), blocks(coarse, size))
        ]
        if degree < STEPS:
            r = [a + b for a, b in zip(r, back_step(kt, blocks(cur, size), mat, geo))]
        put(cur, r)
        q = blocks(q1, size, (degree - 1) * VARS * size)
        grads = [a + b for a, b in zip(grads, star_grads(blocks(cur, size), q))]
    for copy in sent2:
        copy.wait()

    outer_faces(raw, rx2, slot, turn, tn, outer2, elems)
    change = surface(lf, own2, outer2, mat, geo, elems)
    put(final, [
        s + m + c for s, m, c in zip(blocks(middle, size), blocks(final, size), change)
    ])
    more = update_grads(seed2, lt, own2, outer2, qu2, mat, geo, elems)
    grad[...] = jnp.concatenate([a + b for a, b in zip(grads, more)], axis=0)


def body(
    start_state, material, geometry, clusters, neighbours, orientation,
    stiffness, face_trace, face_lift, face_turns, cotangent,
):
    rows, elems = start_state.shape
    basis = rows // VARS
    devices = lax.axis_size("dom")
    fb = -(-face_trace.shape[1] // 8) * 8
    frows = -(-(VARS * fb + 1) // 128) * 128
    full, faces, slots = (rows, elems), (frows, 4 * elems), (SLOTS, frows)
    hist = (STEPS * rows, elems)
    args = (
        start_state, cotangent, material, geometry, clusters.reshape(1, elems), neighbours,
        orientation, stiffness, face_trace, face_lift, face_turns,
    )
    scratch = [full] * 12 + [hist] * 3 + [faces] * 7 + [slots] * 8
    scratch += [(4, fb, basis), (4, fb, basis), (3, fb, fb), (3, fb, fb)]
    return pl.pallas_call(
        functools.partial(step_kernel, devices),
        out_shape=[
            jax.ShapeDtypeStruct((rows, elems), f32),
            jax.ShapeDtypeStruct((3, elems), f32),
        ],
        in_specs=[pl.BlockSpec(memory_space=pltpu.VMEM)] * len(args),
        out_specs=[pl.BlockSpec(memory_space=pltpu.VMEM)] * 2,
        scratch_shapes=[pltpu.VMEM(s, f32) for s in scratch]
        + [pltpu.VMEM((4, elems), jnp.int32)] * 3
        + [pltpu.SemaphoreType.DMA((4 * LANES,))] * 2,
        compiler_params=pltpu.CompilerParams(
            vmem_limit_bytes=60000 * 1024, collective_id=0, has_side_effects=True
        ),
        name="ader_step",
    )(*args)


def solution(mesh):
    return jax.shard_map(
        body,
        mesh=mesh,
        in_specs=(
            P(None, "dom"),
            P(None, "dom"),
            P(None, "dom"),
            P("dom"),
            P(None, "dom"),
            P(None, "dom"),
            P(),
            P(),
            P(),
            P(),
            P(None, "dom"),
        ),
        out_specs=(P(None, "dom"), P(None, "dom")),
        check_vma=False,
    )
```

```python
import functools

import jax
import jax.numpy as jnp
from jax import lax
from jax.experimental import pallas as pl
from jax.experimental.pallas import tpu as pltpu
from jax.sharding import PartitionSpec as P

VARS = 9
TERMS = 6
REACH = 4
CAP = 16
LANES = 2 * REACH + 1
SLOTS = LANES * CAP
STEPS = TERMS - 1
f32, bf16 = jnp.float32, jnp.bfloat16

dt_step = 0.5
root_third = 0.5773502691896258
face_normals = (
    (0.0, 0.0, -1.0),
    (0.0, -1.0, 0.0),
    (-1.0, 0.0, 0.0),
    (root_third, root_third, root_third),
)


def taylor_weights(start_time, length):
    weights = []
    factorial = 1.0
    for degree in range(TERMS):
        factorial = factorial * (degree + 1)
        weights.append(
            ((start_time + length) ** (degree + 1) - start_time ** (degree + 1)) / factorial
        )
    return weights


A_W = taylor_weights(0.0, 0.5 * dt_step)
C_W = taylor_weights(0.5 * dt_step, 0.5 * dt_step)


def right3(x):
    high = x.astype(bf16).astype(f32)
    return jnp.concatenate([high, high, x - high], axis=0).astype(bf16)


def left3(a):
    high = a.astype(bf16).astype(f32)
    return jnp.concatenate([high, a - high, high], axis=1).astype(bf16)


def halves(x):
    high = x.astype(bf16)
    return high, (x - high.astype(f32)).astype(bf16)


def mm(a, b):
    return jnp.dot(a, b, preferred_element_type=f32)


def mm_t(a, b):
    return lax.dot_general(a, b, (((1,), (1,)), ((), ())), preferred_element_type=f32)


def add(*terms):
    total = None
    for t in terms:
        if t is not None:
            total = t if total is None else total + t
    return total


def times(a, b):
    return None if a is None or b is None else a * b


def star_q(a):
    return [
        a(0, 6),
        a(1, 7),
        a(2, 8),
        add(a(0, 7), a(1, 6)),
        add(a(1, 8), a(2, 7)),
        add(a(0, 8), a(2, 6)),
        add(a(0, 0), a(1, 3), a(2, 5)),
        add(a(0, 3), a(1, 1), a(2, 4)),
        add(a(0, 5), a(1, 4), a(2, 2)),
    ]


def star_rows(q, mat):
    lam, mu, rinv = mat
    spread = lam * add(q[0], q[1], q[2])
    rows = [add(spread, times(2.0 * mu, q[v])) for v in range(3)]
    rows += [times(mu, q[v]) for v in range(3, 6)]
    rows += [times(rinv, q[v]) for v in range(6, 9)]
    return rows


def star_back(z, mat):
    lam, mu, rinv = mat

    def normal(axis):
        own = z(axis, axis)
        if own is None:
            return None
        return lam * (z(axis, 0) + z(axis, 1) + z(axis, 2)) + 2.0 * mu * own

    return [
        times(rinv, z(0, 6)),
        times(rinv, z(1, 7)),
        times(rinv, z(2, 8)),
        times(rinv, add(z(0, 7), z(1, 6))),
        times(rinv, add(z(1, 8), z(2, 7))),
        times(rinv, add(z(0, 8), z(2, 6))),
        add(normal(0), times(mu, add(z(1, 3), z(2, 5)))),
        add(normal(1), times(mu, add(z(0, 3), z(2, 4)))),
        add(normal(2), times(mu, add(z(1, 4), z(0, 5)))),
    ]


def star_grads(r, q):
    g_lam = (r[0] + r[1] + r[2]) * add(q[0], q[1], q[2])
    g_mu = add(*[times(r[v], q[v]) for v in range(3)])
    g_mu = 2.0 * g_mu + 0.0
    g_mu = add(g_mu, *[times(r[v], q[v]) for v in range(3, 6)])
    g_r = add(*[times(r[v], q[v]) for v in range(6, 9)])
    return [jnp.sum(g, axis=0, keepdims=True) for g in (g_lam, g_mu, g_r)]


def rows_of(ref, count):
    return [ref[n : n + 1, :] for n in range(count)]


def blocks(ref, size, base=0):
    return [ref[base + v * size : base + (v + 1) * size, :] for v in range(VARS)]


def put(ref, values, base=0):
    size = values[0].shape[0]
    for v in range(VARS):
        ref[base + v * size : base + (v + 1) * size, :] = values[v]


def pieces(matrix, values, geo):
    size = values[0].shape[0]
    products = [mm(matrix, right3(x)) for x in values]
    return lambda axis, v: geo[axis] * products[v][axis * size : (axis + 1) * size]


def predict_steps(matrix, start, states, mat, geo, outs):
    size = start.shape[0] // VARS
    count = VARS * size
    for degree in range(1, TERMS):
        cur = blocks(start, size) if degree == 1 else blocks(states, size, (degree - 2) * count)
        new = star_rows(star_q(pieces(matrix, cur, geo)), mat)
        put(states, new, (degree - 1) * count)
    for v in range(VARS):
        rows = slice(v * size, (v + 1) * size)
        terms = [start[rows, :]]
        terms += [
            states[k * count + v * size : k * count + (v + 1) * size, :] for k in range(STEPS)
        ]
        for ref, weights in outs:
            ref[rows, :] = add(*[w * t for w, t in zip(weights, terms)])


def state_sums(r, x):
    mixed = (r[0] + r[1] + r[2]) * (x[0] + x[1] + x[2])
    groups = [add(*[r[v] * x[v] for v in range(g, g + 3)]) for g in (0, 3, 6)]
    return [jnp.sum(g, axis=0, keepdims=True) for g in [mixed] + groups]


def sums_to_grads(sums, mat):
    lam, mu, rinv = mat
    g_lam = sums[0] / (3.0 * lam + 2.0 * mu)
    return [g_lam, (sums[1] - lam * g_lam + sums[2]) / mu, sums[3] / rinv]


def back_step(matrix_t, r, mat, geo):
    return star_back(pieces(matrix_t, r, geo), mat)


def chain_sums(hist_ref, states, size):
    total = None
    for degree in range(STEPS):
        base = degree * VARS * size
        more = state_sums(blocks(hist_ref, size, base), blocks(states, size, base))
        total = more if total is None else [a + b for a, b in zip(total, more)]
    return total


def trace_faces(tr, window, own_ref, elems):
    size = window.shape[0] // VARS
    fb = tr.shape[0] // 4
    for v in range(VARS):
        t = mm(tr, right3(window[v * size : (v + 1) * size, :]))
        for g in range(4):
            own_ref[v * fb : (v + 1) * fb, g * elems : (g + 1) * elems] = t[g * fb : (g + 1) * fb]
    if own_ref.shape[0] > VARS * fb:
        own_ref[VARS * fb :, :] = jnp.zeros(
            (own_ref.shape[0] - VARS * fb, own_ref.shape[1]), f32
        )


def onehot(rows, row_index):
    at = lax.broadcasted_iota(jnp.int32, (rows, row_index.shape[1]), 0)
    return jnp.where(at == row_index, 1.0, 0.0).astype(bf16)


def serve_hot(arrived, g, elems):
    at = lax.broadcasted_iota(jnp.int32, (SLOTS, elems), 1) + (g * elems + 1)
    return jnp.where(at == arrived, 1.0, 0.0).astype(bf16)


def serve(own_ref, arr_ref, tx_ref, elems):
    arrived = arr_ref[:, arr_ref.shape[1] - 1 :].astype(jnp.int32)
    total = None
    for g in range(4):
        hot = serve_hot(arrived, g, elems)
        high, low = halves(own_ref[:, g * elems : (g + 1) * elems])
        part = mm_t(hot, high) + mm_t(hot, low)
        total = part if total is None else total + part
    tx_ref[...] = total


def padded_t(rx_ref):
    x = rx_ref[...]
    pad = -x.shape[0] % 128
    return jnp.concatenate([x, jnp.zeros((pad, x.shape[1]), f32)], axis=0).T


def masked3(x, turn_row):
    return right3(jnp.concatenate([jnp.where(turn_row == o, x, 0.0) for o in range(3)], axis=0))


def local_faces(own_ref, idx_ref, raw_ref, elems):
    high, low = halves(own_ref[...])
    for f in range(4):
        hot = onehot(own_ref.shape[1], idx_ref[f : f + 1, :])
        raw_ref[:, f * elems : (f + 1) * elems] = mm(high, hot) + mm(low, hot)


def outer_faces(raw_ref, rx_ref, slot_ref, turn_ref, tn, outer_ref, elems):
    fb = tn.shape[0]
    rx_high, rx_low = halves(padded_t(rx_ref))
    for f in range(4):
        cols = slice(f * elems, (f + 1) * elems)
        hot_s = onehot(rx_high.shape[1], slot_ref[f : f + 1, :])
        raw = raw_ref[:, cols] + mm(rx_high, hot_s) + mm(rx_low, hot_s)
        turn = turn_ref[f : f + 1, :]
        for v in range(VARS):
            outer_ref[v * fb : (v + 1) * fb, cols] = mm(
                tn, masked3(raw[v * fb : (v + 1) * fb], turn)
            )


def face_block(ref, f, elems, fb):
    return [ref[v * fb : (v + 1) * fb, f * elems : (f + 1) * elems] for v in range(VARS)]


def face_q(f, own, far, geo):
    n = [s * g if s else None for s, g in zip(face_normals[f], geo)]
    mean = [0.5 * (a + b) for a, b in zip(own, far)]
    return n, star_q(lambda axis, v: times(n[axis], mean[v]))


def volume(window, kt, mat, geo, q_ref, change_ref):
    size = window.shape[0] // VARS
    q = star_q(pieces(kt, blocks(window, size), geo))
    put(q_ref, q)
    put(change_ref, [-x for x in star_rows(q, mat)])


def surface(lf, own_ref, outer_ref, mat, geo, elems):
    fb = lf.shape[1] // 12
    half_speed = 0.5 * jnp.sqrt((mat[0] + 2.0 * mat[1]) * mat[2])
    flux = [[] for _ in range(VARS)]
    for f in range(4):
        own, far = face_block(own_ref, f, elems, fb), face_block(outer_ref, f, elems, fb)
        rows = star_rows(face_q(f, own, far, geo)[1], mat)
        for v in range(VARS):
            jump = half_speed * (own[v] - far[v])
            flux[v].append(jump if rows[v] is None else jump - rows[v])
    return [-mm(lf, right3(jnp.concatenate(x, axis=0))) for x in flux]


def volume_back(seed, ks, mat, geo):
    return [-x for x in star_back(pieces(ks, seed, geo), mat)]


def faces_cot(seed, lt, tnt, idx_ref, slot_ref, turn_ref, mat, geo, own_cot, tx_ref, elems):
    fb = lt.shape[0] // 4
    lam, mu, rinv = mat
    half_speed = 0.5 * jnp.sqrt((lam + 2.0 * mu) * rinv)
    lifted = [-mm(lt, right3(s)) for s in seed]
    pad = own_cot.shape[0] - VARS * fb
    scattered, sent = None, None
    for f in range(4):
        n = [s * g if s else None for s, g in zip(face_normals[f], geo)]
        r = [lifted[v][f * fb : (f + 1) * fb] for v in range(VARS)]
        back = star_back(lambda axis, v: times(n[axis], r[v]), mat)
        turn = turn_ref[f : f + 1, :]
        raw = []
        for v in range(VARS):
            side = half_speed * r[v]
            mean = jnp.zeros_like(side) if back[v] is None else -0.5 * back[v]
            own_cot[v * fb : (v + 1) * fb, f * elems : (f + 1) * elems] = mean + side
            raw.append(mm(tnt, masked3(mean - side, turn)))
        raw = jnp.concatenate(raw + [jnp.zeros((pad, elems), f32)], axis=0)
        high, low = halves(raw)
        hot = onehot(own_cot.shape[1], idx_ref[f : f + 1, :])
        hot_s = onehot(SLOTS, slot_ref[f : f + 1, :])
        part = mm_t(high, hot) + mm_t(low, hot)
        scattered = part if scattered is None else scattered + part
        part = mm_t(hot_s, high) + mm_t(hot_s, low)
        sent = part if sent is None else sent + part
    tx_ref[...] = sent
    own_cot[VARS * fb :, :] = jnp.zeros((pad, own_cot.shape[1]), f32)
    own_cot[...] = own_cot[...] + scattered


def update_grads(seed, lt, own_ref, outer_ref, q_ref, mat, geo, elems):
    fb = lt.shape[0] // 4
    grads = [-g for g in star_grads(seed, blocks(q_ref, seed[0].shape[0]))]
    lam, mu, rinv = mat
    speed = jnp.sqrt((lam + 2.0 * mu) * rinv)
    g_speed = jnp.zeros_like(lam)
    lifted = [-mm(lt, right3(s)) for s in seed]
    for f in range(4):
        own, far = face_block(own_ref, f, elems, fb), face_block(outer_ref, f, elems, fb)
        q = face_q(f, own, far, geo)[1]
        r = [lifted[v][f * fb : (f + 1) * fb] for v in range(VARS)]
        grads = [a - b for a, b in zip(grads, star_grads(r, q))]
        jump = add(*[r[v] * (own[v] - far[v]) for v in range(VARS)])
        g_speed = g_speed + 0.5 * jnp.sum(jump, axis=0, keepdims=True)
    return [
        grads[0] + g_speed * rinv / (2.0 * speed),
        grads[1] + g_speed * rinv / speed,
        grads[2] + g_speed * (lam + 2.0 * mu) / (2.0 * speed),
    ]


def faces_back(own_cot, rx_ref, arr_ref, trt, elems):
    fb = trt.shape[1] // 12
    arrived = arr_ref[:, arr_ref.shape[1] - 1 :].astype(jnp.int32)
    rx = padded_t(rx_ref)[:, :SLOTS]
    high, low = halves(rx)
    total = []
    for g in range(4):
        hot = serve_hot(arrived, g, elems)
        total.append(
            own_cot[:, g * elems : (g + 1) * elems] + mm(high, hot) + mm(low, hot)
        )
    return [
        mm(trt, right3(jnp.concatenate([t[v * fb : (v + 1) * fb] for t in total], axis=0)))
        for v in range(VARS)
    ]


def peers_of(devices):
    me = lax.axis_index("dom")
    shifts = [n + 1 for n in range(REACH)] + [-(n + 1) for n in range(REACH)] + [devices // 2]
    return [
        [lax.rem(me + sign * s + 2 * devices, devices) for s in shifts] for sign in (1, -1)
    ]


def send_all(peers, src, dst, send_sems, recv_sems, base=0):
    copies = []
    for n in reversed(range(LANES)):
        rows = pl.ds(n * CAP, CAP)
        copy = pltpu.make_async_remote_copy(
            src_ref=src.at[rows],
            dst_ref=dst.at[rows],
            send_sem=send_sems.at[base + n],
            recv_sem=recv_sems.at[base + n],
            device_id=(peers[n],),
            device_id_type=pl.DeviceIdType.MESH,
        )
        copy.start()
        copies.append(copy)
    return copies


def face_places(neighbours, orientation, devices, idx_ref, slot_ref, turn_ref):
    elems = neighbours.shape[1]
    me = lax.axis_index("dom")
    at = lax.broadcasted_iota(jnp.int32, (16, elems), 0)
    col = lax.broadcasted_iota(jnp.int32, (16, elems), 1)
    rows = lax.broadcasted_iota(jnp.int32, (SLOTS, elems), 0)
    carry = jnp.zeros((16, 1), jnp.int32)
    total = jnp.zeros((SLOTS, 1), jnp.int32)
    for f in range(4):
        name, code = neighbours[f : f + 1, :], orientation[f : f + 1, :]
        far_face = sum(jnp.where(code >= 3 * g, 1, 0) for g in (1, 2, 3))
        turn_ref[f : f + 1, :] = code - 3 * far_face
        present = name >= 0
        safe = jnp.maximum(name, 0)
        owner = jnp.floor((safe.astype(f32) + 0.5) * (1.0 / elems)).astype(jnp.int32)
        source = far_face * elems + safe - owner * elems
        away = owner - me
        away = jnp.where(away < 0, away + devices, away)
        idx_ref[f : f + 1, :] = jnp.where(present & (away == 0), source, -1)
        lane = jnp.where(
            away <= REACH,
            away - 1,
            jnp.where(away >= devices - REACH, REACH + devices - away - 1, 2 * REACH),
        )
        lane = jnp.where(present & (away != 0), lane, LANES)
        hot = jnp.where(at == lane, 1, 0)
        run = hot
        shift = 1
        while shift < elems:
            run = run + jnp.where(col >= shift, pltpu.roll(run, shift, 1), 0)
            shift *= 2
        rank = jnp.sum((run + carry - 1) * hot, axis=0, keepdims=True)
        carry = carry + jnp.sum(hot, axis=1, keepdims=True)
        slot = jnp.where(lane < LANES, lane * CAP + rank, -1)
        slot_ref[f : f + 1, :] = slot
        total = total + jnp.sum(jnp.where(rows == slot, source + 1, 0), axis=1, keepdims=True)
    return total


def stacked(blocks_in, scratch):
    scratch[...] = jnp.zeros(scratch.shape, f32)
    for n, x in enumerate(blocks_in):
        scratch[n, : x.shape[0], : x.shape[1]] = x
    return jnp.concatenate([scratch[n] for n in range(scratch.shape[0])], axis=0)


def step_kernel(
    devices,
    state, cot, mat_ref, geo_ref, fine, neighbours, orientation, stiffness, face_trace,
    face_lift, face_turns,
    final, grad,
    w1, wc, w2, cur, part, middle, coarse, seed1, direct1, direct2, qu1, qu2,
    q1, q2, hist, own1, own2, own_cot1, own_cot2, raw, outer1, outer2,
    tx0, tx1, tx2, tx3, rx0, rx1, rx2, rx3, trace_pad, lift_pad, turn_pad, turn_pad_t,
    idx, slot, turn, send_sems, recv_sems,
):
    up, down = peers_of(devices)
    barrier = pltpu.get_barrier_semaphore()
    for peer in up:
        pl.semaphore_signal(
            barrier, inc=1, device_id=(peer,), device_id_type=pl.DeviceIdType.MESH
        )
    elems = state.shape[1]
    size = state.shape[0] // VARS
    mat, geo = rows_of(mat_ref, 3), rows_of(geo_ref, 3)
    total = face_places(neighbours, orientation, devices, idx, slot, turn)

    stiff = [stiffness[d] for d in range(3)]
    ks = left3(jnp.concatenate(stiff, axis=0))
    kt = left3(jnp.concatenate([x.T for x in stiff], axis=0))
    trace = stacked([face_trace[:, g, :] for g in range(4)], trace_pad)
    lift = stacked([face_lift[:, f, :] for f in range(4)], lift_pad)
    tr, trt, lt, lf = left3(trace), left3(trace.T), left3(lift), left3(lift.T)
    tnt = left3(stacked([face_turns[o] for o in range(3)], turn_pad).T)
    tn = left3(stacked([face_turns[o].T for o in range(3)], turn_pad_t).T)

    seed2 = blocks(cot, size)
    faces_cot(seed2, lt, tnt, idx, slot, turn, mat, geo, own_cot2, tx0, elems)
    last = lax.broadcasted_iota(jnp.int32, tx0.shape, 1) == tx0.shape[1] - 1
    tx0[...] = jnp.where(last, total.astype(f32), tx0[...])
    pl.semaphore_wait(barrier, LANES)
    sent0 = send_all(up, tx0, rx0, send_sems, recv_sems, 0)

    predict_steps(ks, state, q1, mat, geo, [(w1, A_W), (wc, C_W)])
    trace_faces(tr, w1, own1, elems)
    local_faces(own1, idx, raw, elems)
    volume(w1, kt, mat, geo, qu1, middle)
    put(direct2, volume_back(seed2, ks, mat, geo))
    for copy in sent0:
        copy.wait()

    serve(own1, rx0, tx1, elems)
    back = faces_back(own_cot2, rx0, rx0, trt, elems)
    is_fine = fine[...] == 1
    for v, (b, d) in enumerate(zip(back, blocks(direct2, size))):
        rows = slice(v * size, (v + 1) * size)
        part[rows, :] = jnp.where(is_fine, b + d, 0.0)
        coarse[rows, :] = jnp.where(is_fine, 0.0, b + d)
    sent1 = send_all(down, tx1, rx1, send_sems, recv_sems, LANES)

    put(hist, [A_W[STEPS] * x for x in blocks(part, size)], (STEPS - 1) * VARS * size)
    for degree in range(STEPS, 0, -1):
        r = back_step(kt, blocks(hist, size, (degree - 1) * VARS * size), mat, geo)
        r = [a + A_W[degree - 1] * b for a, b in zip(r, blocks(part, size))]
        if degree > 1:
            put(hist, r, (degree - 2) * VARS * size)
        else:
            put(seed1, [a + b for a, b in zip(r, blocks(cot, size))])
    faces_cot(
        blocks(seed1, size), lt, tnt, idx, slot, turn, mat, geo, own_cot1, tx3, elems
    )
    put(direct1, volume_back(blocks(seed1, size), ks, mat, geo))
    sent3 = send_all(up, tx3, rx3, send_sems, recv_sems, 2 * LANES)
    for copy in sent1:
        copy.wait()

    outer_faces(raw, rx1, slot, turn, tn, outer1, elems)
    change = surface(lf, own1, outer1, mat, geo, elems)
    put(middle, [
        s + m + c for s, m, c in zip(blocks(state, size), blocks(middle, size), change)
    ])
    predict_steps(ks, middle, q2, mat, geo, [(w2, A_W)])
    w2[...] = jnp.where(is_fine, w2[...], wc[...])
    trace_faces(tr, w2, own2, elems)
    serve(own2, rx0, tx2, elems)
    local_faces(own2, idx, raw, elems)
    sent2 = send_all(down, tx2, rx2, send_sems, recv_sems, 3 * LANES)

    volume(w2, kt, mat, geo, qu2, final)
    grads = update_grads(blocks(seed1, size), lt, own1, outer1, qu1, mat, geo, elems)
    sums = chain_sums(hist, q2, size)
    for copy in sent3:
        copy.wait()
    back = faces_back(own_cot1, rx3, rx0, trt, elems)
    put(part, [a + b for a, b in zip(back, blocks(direct1, size))])
    for degree in range(STEPS, 0, -1):
        r = [
            A_W[degree] * a + C_W[degree] * b
            for a, b in zip(blocks(part, size), blocks(coarse, size))
        ]
        if degree < STEPS:
            r = [a + b for a, b in zip(r, back_step(kt, blocks(cur, size), mat, geo))]
        put(cur, r)
        q = blocks(q1, size, (degree - 1) * VARS * size)
        sums = [a + b for a, b in zip(sums, state_sums(blocks(cur, size), q))]
    grads = [a + b for a, b in zip(grads, sums_to_grads(sums, mat))]
    for copy in sent2:
        copy.wait()

    outer_faces(raw, rx2, slot, turn, tn, outer2, elems)
    change = surface(lf, own2, outer2, mat, geo, elems)
    put(final, [
        s + m + c for s, m, c in zip(blocks(middle, size), blocks(final, size), change)
    ])
    more = update_grads(seed2, lt, own2, outer2, qu2, mat, geo, elems)
    grad[...] = jnp.concatenate([a + b for a, b in zip(grads, more)], axis=0)


def body(
    start_state, material, geometry, clusters, neighbours, orientation,
    stiffness, face_trace, face_lift, face_turns, cotangent,
):
    rows, elems = start_state.shape
    basis = rows // VARS
    devices = lax.axis_size("dom")
    fb = -(-face_trace.shape[1] // 8) * 8
    frows = -(-(VARS * fb + 1) // 128) * 128
    full, faces, slots = (rows, elems), (frows, 4 * elems), (SLOTS, frows)
    hist = (STEPS * rows, elems)
    args = (
        start_state, cotangent, material, geometry, clusters.reshape(1, elems), neighbours,
        orientation, stiffness, face_trace.transpose(1, 0, 2), face_lift.transpose(2, 0, 1),
        face_turns,
    )
    scratch = [full] * 12 + [hist] * 3 + [faces] * 7 + [slots] * 8
    scratch += [(4, fb, basis), (4, fb, basis), (3, fb, fb), (3, fb, fb)]
    return pl.pallas_call(
        functools.partial(step_kernel, devices),
        out_shape=[
            jax.ShapeDtypeStruct((rows, elems), f32),
            jax.ShapeDtypeStruct((3, elems), f32),
        ],
        in_specs=[pl.BlockSpec(memory_space=pltpu.VMEM)] * len(args),
        out_specs=[pl.BlockSpec(memory_space=pltpu.VMEM)] * 2,
        scratch_shapes=[pltpu.VMEM(s, f32) for s in scratch]
        + [pltpu.VMEM((4, elems), jnp.int32)] * 3
        + [pltpu.SemaphoreType.DMA((4 * LANES,))] * 2,
        compiler_params=pltpu.CompilerParams(
            vmem_limit_bytes=60000 * 1024, collective_id=0, has_side_effects=True
        ),
        name="ader_step",
    )(*args)


def solution(mesh):
    return jax.shard_map(
        body,
        mesh=mesh,
        in_specs=(
            P(None, "dom"),
            P(None, "dom"),
            P(None, "dom"),
            P("dom"),
            P(None, "dom"),
            P(None, "dom"),
            P(),
            P(),
            P(),
            P(),
            P(None, "dom"),
        ),
        out_specs=(P(None, "dom"), P(None, "dom")),
        check_vma=False,
    )
```
